256 devices in a mesh: depth: 8 (over z_hi, core), seq: 32 (over x, y, z_lo).
Axes of the slice: x: 4, y: 4, z: 8 (z_hi: 4, z_lo: 2; z = z_hi * 2 + z_lo), core: 2. Of those that a mesh axis runs over, the one named last changes fastest.
Arguments:
- queries: bfloat16 [8, 4096, 4096], P('depth', 'seq'), may hold values from -27 to 27
- grad_out: bfloat16 [8, 4096, 4096], P('depth', 'seq'), may hold values from -48 to 48
- key_states: bfloat16 [4096, 4096], P('depth', 'seq'), may hold values from -3 to 3
- value_states: bfloat16 [4096, 4096], P('depth', 'seq'), may hold values from -6 to 6
- offsets: int32 [8], replicated, may hold values from 0 to 8, as said below
- windows: int32 [8], replicated, may hold values from 512 to 1024, as said below
Outputs:
- grad_queries: bfloat16 [8, 4096, 4096], P('depth', 'seq')
- grad_keys: bfloat16 [4096, 4096], P('depth', 'seq')
- grad_values: bfloat16 [4096, 4096], P('depth', 'seq')
The draws below stay inside these ranges and needn't reach their ends.
Inputs may be any that keep to these rules, and one draw needn't show every extreme that they name: `windows`: one depth's window is exactly 1024. `offsets`: one depth's offset is exactly 8.
All inputs are finite; a program needn't handle non-finite values.
Results may differ from the reference program's by a relative error of at most 0.033.
Values may be sent and summed in bfloat16 or wider, within the bound.
A program may use at most 64 MiB of HBM per device.

```python
import math
import jax
import jax.numpy as jnp
from jax import lax

HEADS = 32
HEAD_DIM = 128
MODEL = 4096
DEPTHS = 8
SEQ_LEN = 4096
WIN = 1024
OFF_MAX = 8


def base_keys(key):
    table = jnp.clip(jax.random.normal(jax.random.fold_in(key, 41), (SEQ_LEN, MODEL), jnp.float32), -3.0, 3.0)
    return table


def draw_key_states(key, part):
    return base_keys(key).astype(jnp.bfloat16)


def draw_queries(key, part):
    table = jnp.clip(jax.random.normal(jax.random.fold_in(key, 51), (DEPTHS, SEQ_LEN, MODEL), jnp.float32), -4.0, 4.0)
    return table.astype(jnp.bfloat16)


def draw_offsets(key, part):
    drawn = jax.random.randint(jax.random.fold_in(key, 61), (DEPTHS,), 0, OFF_MAX + 1)
    chosen = jax.random.randint(jax.random.fold_in(key, 62), (), 0, DEPTHS)
    return drawn.at[chosen].set(OFF_MAX)


def draw_windows(key, part):
    drawn = jax.random.randint(jax.random.fold_in(key, 71), (DEPTHS,), WIN // 2, WIN + 1)
    chosen = jax.random.randint(jax.random.fold_in(key, 72), (), 0, DEPTHS)
    return drawn.at[chosen].set(WIN)


def block_scale(key, dims, shards, smallest, top_value):
    def one(position, shards_of):
        draws = jax.random.uniform(jax.random.fold_in(jax.random.fold_in(key, 6), position), (shards_of,), jnp.float32, smallest / len(shards), top_value / len(shards))
        return jnp.repeat(jnp.exp(draws), dims[position] // shards_of).reshape((-1,) + (1,) * (len(dims) - position - 1))

    gain = one(*shards[0])
    for cut in shards[1:]:
        gain = gain * one(*cut)
    return gain


def scatter_about(rng, dims, scale, limit, split=(), held_as=jnp.bfloat16):
    values = scale * jax.random.normal(rng, dims, jnp.float32)
    if split:
        values = values * block_scale(rng, dims, split, -0.22, 0.18)
    return jnp.clip(values, -limit, limit).astype(held_as)


def setup_inputs(seed: int = 0) -> dict:
    key_of = jax.random.split(jax.random.key(seed), 7)
    return {
        "queries": draw_queries(jax.random.fold_in(key_of[6], 71), 0),
        "grad_out": scatter_about(key_of[1], (DEPTHS, SEQ_LEN, MODEL), 8.0, 48.0, ((0, 8), (1, 32))),
        "key_states": draw_key_states(jax.random.fold_in(key_of[6], 71), 0),
        "value_states": scatter_about(key_of[3], (SEQ_LEN, MODEL), 1.0, 6.0, ((0, 8), (1, 32))),
        "offsets": draw_offsets(jax.random.fold_in(key_of[6], 71), 0),
        "windows": draw_windows(jax.random.fold_in(key_of[6], 71), 0),
    }


def allowed_mask(query_pos, key_pos, shift_now, span_now, seq_total):
    query_col = query_pos[:, None]
    key_row = key_pos[None, :]
    inside = (key_row >= 0) & (key_row < seq_total) & (query_col >= 0) & (query_col < seq_total)
    return inside & (key_row <= query_col + shift_now) & (key_row > query_col + shift_now - span_now)

def rounded(values_in):
    return lax.optimization_barrier(values_in.astype(jnp.bfloat16)).astype(jnp.float32)

def depth_terms(query3, grad3, key_pad, value_pad, shift_now, span_now, block_len):
    scaling = 1.0 / math.sqrt(HEAD_DIM)
    blocks = SEQ_LEN // block_len
    span_keys = block_len + WIN

    def backward(carry, number):
        key_acc, value_acc = carry
        first_row = number * block_len
        key_first = first_row + shift_now + 1
        query_blk = lax.dynamic_slice_in_dim(query3, first_row, block_len, 0).astype(jnp.float32)
        grad_blk = lax.dynamic_slice_in_dim(grad3, first_row, block_len, 0).astype(jnp.float32)
        key_blk = lax.dynamic_slice_in_dim(key_pad, key_first, span_keys, 0).astype(jnp.float32)
        value_blk = lax.dynamic_slice_in_dim(value_pad, key_first, span_keys, 0).astype(jnp.float32)
        scores = jnp.einsum('qhd,khd->hqk', query_blk, key_blk) * scaling
        query_pos = first_row + jnp.arange(block_len, dtype=jnp.int32)
        key_pos = key_first - WIN + jnp.arange(span_keys, dtype=jnp.int32)
        allowed = allowed_mask(query_pos, key_pos, shift_now, span_now, SEQ_LEN)
        masked = jnp.where(allowed[None], scores, -jnp.inf)
        highest = lax.optimization_barrier(jnp.max(masked, axis=2, keepdims=True))
        log_total = highest + jnp.log(lax.optimization_barrier(jnp.sum(jnp.exp(masked - highest), axis=2, keepdims=True)))
        probs = jnp.exp(masked - log_total)
        weights = rounded(probs)
        grad_probs = jnp.einsum('qhd,khd->hqk', grad_blk, value_blk)
        row_dot = lax.optimization_barrier(jnp.sum(weights * grad_probs, axis=2, keepdims=True))
        grad_scores = rounded(probs * (grad_probs - row_dot))
        grad_query = jnp.einsum('hqk,khd->qhd', grad_scores, key_blk) * scaling
        key_term = jnp.einsum('hqk,qhd->khd', grad_scores, query_blk) * scaling
        value_term = jnp.einsum('hqk,qhd->khd', weights, grad_blk)
        root = jnp.zeros((), jnp.int32)
        place = (key_first.astype(jnp.int32), root, root)
        key_acc = lax.dynamic_update_slice(key_acc, lax.dynamic_slice(key_acc, place, key_term.shape) + key_term, place)
        value_acc = lax.dynamic_update_slice(value_acc, lax.dynamic_slice(value_acc, place, value_term.shape) + value_term, place)
        return ((key_acc, value_acc), grad_query)
    padded_len = SEQ_LEN + WIN + OFF_MAX + 1
    start_acc = jnp.zeros((padded_len, HEADS, HEAD_DIM), jnp.float32)
    (key_acc, value_acc), grad_rows = lax.scan(backward, (start_acc, start_acc), jnp.arange(blocks, dtype=jnp.int32))
    grad_query = grad_rows.reshape(SEQ_LEN, MODEL)
    key_part = key_acc[WIN:WIN + SEQ_LEN].reshape(SEQ_LEN, MODEL)
    value_part = value_acc[WIN:WIN + SEQ_LEN].reshape(SEQ_LEN, MODEL)
    return (grad_query, key_part, value_part)

def reference(queries, grad_out, key_states, value_states, offsets, windows):
    block_len = min(512, SEQ_LEN // DEPTHS)
    widths = ((WIN, OFF_MAX + 1), (0, 0), (0, 0))
    key_pad = jnp.pad(key_states.reshape(SEQ_LEN, HEADS, HEAD_DIM), widths)
    value_pad = jnp.pad(value_states.reshape(SEQ_LEN, HEADS, HEAD_DIM), widths)
    grad_list = []
    key_sum = jnp.zeros((SEQ_LEN, MODEL), jnp.float32)
    value_sum = jnp.zeros((SEQ_LEN, MODEL), jnp.float32)
    for depth_id in range(DEPTHS):
        query3 = queries[depth_id].reshape(SEQ_LEN, HEADS, HEAD_DIM)
        grad3 = grad_out[depth_id].reshape(SEQ_LEN, HEADS, HEAD_DIM)
        grad_query, key_part, value_part = depth_terms(query3, grad3, key_pad, value_pad, offsets[depth_id], windows[depth_id], block_len)
        grad_list.append(grad_query.astype(jnp.bfloat16))
        key_sum = key_sum + rounded(key_part)
        value_sum = value_sum + rounded(value_part)
    return (jnp.stack(grad_list), key_sum.astype(jnp.bfloat16), value_sum.astype(jnp.bfloat16))
```

```python
import functools
import math

import jax
import jax.numpy as jnp
from jax import lax
from jax.experimental import pallas as pl
from jax.experimental.pallas import tpu as pltpu
from jax.sharding import PartitionSpec as P

HEAD_DIM = 128
WIN = 1024
TILE = 256
SPAN = WIN + TILE
NEG = -1e30
SCALE = 1.0 / math.sqrt(HEAD_DIM)
SCALE2 = SCALE * math.log2(math.e)


def dot_t(a, b):
    return lax.dot_general(a, b, (((1,), (1,)), ((), ())), preferred_element_type=jnp.float32)


def attention_kernel(
    scal_ref, q_ref, g_ref, k_ref, v_ref, dq_ref, dkv_ref, stage, ks, vs, kt, dks, dvs, s_scr, dp_scr
):
    shift = scal_ref[0]
    span = scal_ref[1]
    rows = q_ref.shape[0]
    total = rows + WIN

    stage[pl.ds(rows, 16), :] = jnp.zeros((16, HEAD_DIM), jnp.float32)
    for src, dst in ((k_ref, ks), (v_ref, vs)):
        dst[pl.ds(0, WIN - 16), :] = jnp.zeros((WIN - 16, HEAD_DIM), jnp.bfloat16)
        stage[pl.ds(0, rows), :] = src[...].astype(jnp.float32)
        dst[pl.ds(WIN, rows), :] = stage[pl.ds(shift, rows), :].astype(jnp.bfloat16)
        head = stage[pl.ds(0, 16), :]
        wide = jnp.concatenate([jnp.zeros((16, HEAD_DIM), jnp.float32), head], axis=0)
        stage[pl.ds(0, 32), :] = wide
        dst[pl.ds(WIN - 16, 16), :] = stage[pl.ds(shift, 16), :].astype(jnp.bfloat16)
    for c in range(total // TILE):
        kt[:, pl.ds(c * TILE, TILE)] = ks[pl.ds(c * TILE, TILE), :].T
    dks[...] = jnp.zeros_like(dks)
    dvs[...] = jnp.zeros_like(dvs)

    blocks = SPAN // TILE
    gap = lax.broadcasted_iota(jnp.int32, (TILE, TILE), 0) - lax.broadcasted_iota(
        jnp.int32, (TILE, TILE), 1
    )
    row = lax.broadcasted_iota(jnp.int32, (TILE, TILE), 0)

    def tile(t, carry):
        first = pl.multiple_of(t * TILE, TILE)
        q = q_ref[pl.ds(first, TILE), :]
        g = g_ref[pl.ds(first, TILE), :]
        high = jnp.full((1, TILE), NEG, jnp.float32)
        for b in range(blocks):
            at = pl.multiple_of(first + b * TILE, TILE)
            s = dot_t(ks[pl.ds(at, TILE), :], q)
            keep = gap > (WIN - b * TILE) - span
            if b == blocks - 1:
                keep = keep & (gap <= 0)
            pos = row + (at + shift - WIN)
            keep = keep & (pos >= 0) & (pos < rows)
            s = jnp.where(keep, s, NEG)
            s_scr[pl.ds(b * TILE, TILE), :] = s
            high = jnp.maximum(high, jnp.max(s, axis=0, keepdims=True))
        total_e = jnp.zeros((1, TILE), jnp.float32)
        total_d = jnp.zeros((1, TILE), jnp.float32)
        for b in range(blocks):
            at = pl.multiple_of(first + b * TILE, TILE)
            dp = dot_t(vs[pl.ds(at, TILE), :], g)
            e = jnp.exp2((s_scr[pl.ds(b * TILE, TILE), :] - high) * SCALE2)
            total_e += jnp.sum(e, axis=0, keepdims=True)
            total_d += jnp.sum(e * dp, axis=0, keepdims=True)
            s_scr[pl.ds(b * TILE, TILE), :] = e
            dp_scr[pl.ds(b * TILE, TILE), :] = dp
        inv = 1.0 / total_e
        rowdot = total_d * inv
        dqt = jnp.zeros((HEAD_DIM, TILE), jnp.float32)
        for b in range(blocks):
            at = pl.multiple_of(first + b * TILE, TILE)
            p = s_scr[pl.ds(b * TILE, TILE), :] * inv
            ds = (p * (dp_scr[pl.ds(b * TILE, TILE), :] - rowdot)).astype(jnp.bfloat16)
            pb = p.astype(jnp.bfloat16)
            dvs[pl.ds(at, TILE), :] += jnp.dot(pb, g, preferred_element_type=jnp.float32)
            dks[pl.ds(at, TILE), :] += jnp.dot(ds, q, preferred_element_type=jnp.float32)
            dqt += jnp.dot(kt[:, pl.ds(at, TILE)], ds, preferred_element_type=jnp.float32)
        dq_ref[pl.ds(first, TILE), :] = (dqt.T * SCALE).astype(jnp.bfloat16)
        return carry

    lax.fori_loop(0, rows // TILE, tile, 0)

    dkv_ref[:, :HEAD_DIM] = (dks[pl.ds(WIN - shift, rows), :] * SCALE).astype(jnp.bfloat16)
    dkv_ref[:, HEAD_DIM:] = dvs[pl.ds(WIN - shift, rows), :].astype(jnp.bfloat16)


def attention_backward(scalars, q, g, k, v):
    rows = q.shape[0]
    vmem = pl.BlockSpec(memory_space=pltpu.VMEM)
    return pl.pallas_call(
        attention_kernel,
        out_shape=(
            jax.ShapeDtypeStruct((rows, HEAD_DIM), jnp.bfloat16),
            jax.ShapeDtypeStruct((rows, 2 * HEAD_DIM), jnp.bfloat16),
        ),
        in_specs=[pl.BlockSpec(memory_space=pltpu.SMEM)] + [vmem] * 4,
        out_specs=(vmem, vmem),
        scratch_shapes=[
            pltpu.VMEM((rows + 16, HEAD_DIM), jnp.float32),
            pltpu.VMEM((rows + WIN, HEAD_DIM), jnp.bfloat16),
            pltpu.VMEM((rows + WIN, HEAD_DIM), jnp.bfloat16),
            pltpu.VMEM((HEAD_DIM, rows + WIN), jnp.bfloat16),
            pltpu.VMEM((rows + WIN, HEAD_DIM), jnp.float32),
            pltpu.VMEM((rows + WIN, HEAD_DIM), jnp.float32),
            pltpu.VMEM((SPAN, TILE), jnp.float32),
            pltpu.VMEM((SPAN, TILE), jnp.float32),
        ],
        compiler_params=pltpu.CompilerParams(vmem_limit_bytes=48 << 20),
    )(scalars, q, g, k, v)


def on_device(queries, grad_out, key_states, value_states, offsets, windows):
    depth_id = lax.axis_index("depth")
    picked = jnp.arange(offsets.shape[0], dtype=jnp.int32) == depth_id
    shift_now = jnp.sum(jnp.where(picked, offsets, 0))
    span_now = jnp.sum(jnp.where(picked, windows, 0))
    scalars = jnp.stack([shift_now, span_now])
    tok_rows = queries.shape[1]
    model_width = queries.shape[2]
    q, g = (
        lax.all_to_all(a.reshape(tok_rows, model_width), "seq", split_axis=1, concat_axis=0, tiled=True)
        for a in (queries, grad_out)
    )
    k, v = (lax.all_gather(a, "depth", axis=0, tiled=True) for a in (key_states, value_states))
    dq, dkv = attention_backward(scalars, q, g, k, v)
    summed = lax.psum_scatter(dkv, "depth", scatter_dimension=0, tiled=True)
    back = lax.all_to_all(dq, "seq", split_axis=0, concat_axis=1, tiled=True)
    return (
        back.reshape(1, tok_rows, model_width),
        summed[:, :HEAD_DIM],
        summed[:, HEAD_DIM:],
    )


def solution(mesh):
    in_specs = (
        P("depth", "seq", None),
        P("depth", "seq", None),
        P("depth", "seq"),
        P("depth", "seq"),
        P(),
        P(),
    )
    out_specs = (P("depth", "seq", None), P("depth", "seq"), P("depth", "seq"))
    return jax.shard_map(
        on_device, mesh=mesh, in_specs=in_specs, out_specs=out_specs, check_vma=False
    )
```

```python
import functools
import math

import jax
import jax.numpy as jnp
from jax import lax
from jax.experimental import pallas as pl
from jax.experimental.pallas import tpu as pltpu
from jax.sharding import PartitionSpec as P

HD = 128
WIN = 1024
BLK = 128
SIDE = 4
PEERS = SIDE * SIDE
RING = 8
SHARD = 512
TOTAL = 4096
PAD = TOTAL + WIN + BLK
SPAN = WIN + 3 * BLK + 16
TAIL = 1536
NEG = -1e30
SCALE = 1.0 / math.sqrt(HD)
SCALE2 = SCALE * math.log2(math.e)
F32 = jnp.float32
BF16 = jnp.bfloat16
MESH = pl.DeviceIdType.MESH

BLOCKS = (
    (0, 256, "a", "low"),
    (256, 384, "ab", "low"),
    (640, 384, "ab", "low"),
    (1024, 144, "ab", "high"),
    (1168, 112, "b", None),
    (1280, 144, "b", "high"),
)
COLS = {"a": (0, BLK), "b": (BLK, BLK), "ab": (0, 2 * BLK)}
MOVES = (
    (0, 1), (1, 0), (0, 3), (3, 0), (1, 1), (3, 3), (1, 3), (3, 1),
    (0, 2), (2, 0), (2, 1), (1, 2), (2, 3), (3, 2), (2, 2),
)
FLOWS = ((0, 1, 4), (1, -1, 4), (0, -1, 3), (1, 1, 3))


def dot_t(a, b):
    return lax.dot_general(a, b, (((1,), (1,)), ((), ())), preferred_element_type=F32)


def dot(a, b):
    return jnp.dot(a, b, preferred_element_type=F32)


def fused_kernel(
    off_ref, win_ref, q_in, g_in, k_in, v_in,
    dq_out, dk_out, dv_out,
    qg, kv, kt, acc, s_scr, dp_scr, ds_scr, dqs, sib_out, sib_in, ring_out, ring_in,
    x_send, x_recv, own_sem, ag_send, ag_recv, sb_send, sb_recv, dq_send, dq_recv, dq_own,
    ss_send, ss_recv, rs_send, rs_recv,
):
    depth = lax.axis_index("depth")
    seq = lax.axis_index("seq")
    core = depth % 2
    z_lo = seq % 2
    col = seq // 2
    x = col // SIDE
    y = col % SIDE
    z = (depth // 2) * 2 + z_lo

    def at_xy(dx, dy):
        return (depth, (((x + dx) % SIDE) * SIDE + (y + dy) % SIDE) * 2 + z_lo)

    def at_z(to):
        return ((to // 2) * 2 + core, col * 2 + to % 2)

    up = at_z((z + 1) % RING)
    down = at_z((z + RING - 1) % RING)
    sibling = (depth + 1 - 2 * core, seq)

    barrier = pltpu.get_barrier_semaphore()
    partners = [at_xy(*m) for m in MOVES] + [up, down, sibling]
    for dev in partners:
        pl.semaphore_signal(barrier, inc=1, device_id=dev, device_id_type=MESH)
    pl.semaphore_wait(barrier, len(partners))

    def remote(src, dst, send, recv, dev):
        return pltpu.make_async_remote_copy(
            src_ref=src, dst_ref=dst, send_sem=send, recv_sem=recv, device_id=dev, device_id_type=MESH
        )

    def slot(t, origin, side):
        row = pl.multiple_of(WIN + ((origin // 2) * 2 + side) * SHARD, SHARD)
        return kv.at[t, origin % 2, pl.ds(row, SHARD), :]

    own_kv = (k_in, v_in)
    ring = {}
    sent = []
    for f, (t, way, hops) in enumerate(FLOWS):
        c = remote(own_kv[t], slot(t, z, core), ag_send.at[f, 0], ag_recv.at[f, 0], up if way > 0 else down)
        c.start()
        ring[f, 0] = c
    side = {}
    for t in range(2):
        c = remote(own_kv[t], slot(t, z, core), sb_send.at[4, t], sb_recv.at[4, t], sibling)
        c.start()
        side[4, t] = c
    local = []
    for t in range(2):
        c = pltpu.make_async_copy(own_kv[t], slot(t, z, core), own_sem.at[0, t])
        c.start()
        local.append(c)
    mine = pl.multiple_of(col * BLK, BLK)
    exchange = []
    for h in range(2):
        for t, src in enumerate((q_in, g_in)):
            c = pltpu.make_async_copy(
                src.at[:, pl.ds(pl.multiple_of((col * 2 + h) * HD, HD), HD)],
                qg.at[h, t, pl.ds(mine, BLK), :],
                own_sem.at[1 + h, t],
            )
            c.start()
            local.append(c)
            for i, (dx, dy) in enumerate(MOVES):
                to = ((x + dx) % SIDE) * SIDE + (y + dy) % SIDE
                c = remote(
                    src.at[:, pl.ds(pl.multiple_of((to * 2 + h) * HD, HD), HD)],
                    qg.at[h, t, pl.ds(mine, BLK), :],
                    x_send.at[h, t, i],
                    x_recv.at[h, t, i],
                    at_xy(dx, dy),
                )
                c.start()
                exchange.append(c)

    for h in range(2):
        for t in range(2):
            kv[t, h, pl.ds(0, WIN), :] = jnp.zeros((WIN, HD), BF16)
            kv[t, h, pl.ds(WIN + TOTAL, BLK), :] = jnp.zeros((BLK, HD), BF16)
    acc[...] = jnp.zeros_like(acc)
    ds_scr[...] = jnp.zeros_like(ds_scr)

    for hop in range(4):
        for f, (t, way, hops) in enumerate(FLOWS):
            if hop >= hops:
                continue
            ring[f, hop].wait_recv()
            origin = (z + 2 * RING - way * (hop + 1)) % RING
            here = slot(t, origin, core)
            if hop + 1 < hops:
                c = remote(
                    here, here, ag_send.at[f, hop + 1], ag_recv.at[f, hop + 1], up if way > 0 else down
                )
                c.start()
                ring[f, hop + 1] = c
            c = remote(here, here, sb_send.at[f, hop], sb_recv.at[f, hop], sibling)
            c.start()
            side[f, hop] = c
    for c in side.values():
        c.wait_recv()
    for c in local:
        c.wait()
    for c in exchange:
        c.wait_recv()

    for h in range(2):
        def turn(i, carry, h=h):
            row = pl.multiple_of(i * 256, 256)
            kt[h, :, pl.ds(row, 256)] = kv[0, h, pl.ds(row, 256), :].T
            return carry

        lax.fori_loop(0, PAD // 256, turn, 0)
        kt[h, :, pl.ds(PAD - BLK, BLK)] = jnp.zeros((HD, BLK), BF16)

    shift = off_ref[depth]
    span = win_ref[depth]
    lane = lax.broadcasted_iota(jnp.int32, (1, 2 * BLK), 1)
    place = lane + jnp.where(lane >= BLK, BLK, 0)
    last = place + WIN + shift

    def tile(n, carry):
        h = n // 8
        u = n % 8
        base = pl.multiple_of((4 * u + z_lo) * BLK, BLK)
        low = jnp.maximum(last - span, WIN - 1 - base)
        high = jnp.minimum(last, TOTAL + WIN - 1 - base)
        rows_q = pl.multiple_of(u * 2 * BLK, 2 * BLK)
        q = qg[h, 0, pl.ds(rows_q, 2 * BLK), :]
        g = qg[h, 1, pl.ds(rows_q, 2 * BLK), :]

        def join(part, value, halves, op):
            c0, n0 = COLS[halves]
            if halves == "ab":
                return op(part, value)
            if halves == "a":
                return jnp.concatenate([op(part[:, :BLK], value), part[:, BLK:]], axis=1)
            return jnp.concatenate([part[:, :BLK], op(part[:, BLK:], value)], axis=1)

        top = jnp.full((1, 2 * BLK), NEG, F32)
        for k0, rows, halves, bound in BLOCKS:
            c0, cn = COLS[halves]
            at = pl.multiple_of(base + k0, 16)
            s = dot_t(kv[0, h, pl.ds(at, rows), :], q[c0 : c0 + cn])
            if bound is not None:
                key = lax.broadcasted_iota(jnp.int32, (rows, cn), 0)
                if bound == "low":
                    keep = key > low[:, c0 : c0 + cn] - k0
                else:
                    keep = key <= high[:, c0 : c0 + cn] - k0
                s = jnp.where(keep, s, NEG)
            s_scr[pl.ds(k0, rows), pl.ds(c0, cn)] = s
            top = join(top, jnp.max(s, axis=0, keepdims=True), halves, jnp.maximum)
        top = top * SCALE2
        sum_e = jnp.zeros((1, 2 * BLK), F32)
        sum_d = jnp.zeros((1, 2 * BLK), F32)
        for k0, rows, halves, bound in BLOCKS:
            c0, cn = COLS[halves]
            at = pl.multiple_of(base + k0, 16)
            dp = dot_t(kv[1, h, pl.ds(at, rows), :], g[c0 : c0 + cn])
            e = jnp.exp2(s_scr[pl.ds(k0, rows), pl.ds(c0, cn)] * SCALE2 - top[:, c0 : c0 + cn])
            sum_e = join(sum_e, jnp.sum(e, axis=0, keepdims=True), halves, jnp.add)
            sum_d = join(sum_d, jnp.sum(e * dp, axis=0, keepdims=True), halves, jnp.add)
            s_scr[pl.ds(k0, rows), pl.ds(c0, cn)] = e
            dp_scr[pl.ds(k0, rows), pl.ds(c0, cn)] = dp
        inv = 1.0 / sum_e
        rowdot = sum_d * inv
        for k0, rows, halves, bound in BLOCKS:
            c0, cn = COLS[halves]
            at = pl.multiple_of(base + k0, 16)
            p = s_scr[pl.ds(k0, rows), pl.ds(c0, cn)] * inv[:, c0 : c0 + cn]
            ds = p * (dp_scr[pl.ds(k0, rows), pl.ds(c0, cn)] - rowdot[:, c0 : c0 + cn])
            ds = ds.astype(BF16)
            ds_scr[pl.ds(k0, rows), pl.ds(c0, cn)] = ds
            acc[1, h, pl.ds(at, rows), :] += dot(p.astype(BF16), g[c0 : c0 + cn])
            acc[0, h, pl.ds(at, rows), :] += dot(ds, q[c0 : c0 + cn])
        dqt = dot(kt[h, :, pl.ds(base, TAIL)], ds_scr[...])
        dqs[h, pl.ds(rows_q, 2 * BLK), :] = (dqt.T * SCALE).astype(BF16)

        for half in range(2):
            to = 2 * u + half
            src = dqs.at[h, pl.ds(pl.multiple_of(to * BLK, BLK), BLK), :]
            dst = dq_out.at[:, pl.ds(pl.multiple_of((col * 2 + h) * HD, HD), HD)]

            @pl.when(to != col)
            def _():
                remote(src, dst, dq_send.at[h, to], dq_recv.at[h, col], (depth, to * 2 + z_lo)).start()

            @pl.when(to == col)
            def _():
                pltpu.make_async_copy(src, dst, dq_own.at[h]).start()

        return carry

    lax.fori_loop(0, 16, tile, 0)

    scale_of = (SCALE, 1.0)

    def partial(t, target, side):
        row = pl.multiple_of(WIN + ((target // 2) * 2 + side) * SHARD, SHARD)
        value = acc[t, target % 2, pl.ds(row, SHARD), :]
        return value * SCALE if t == 0 else value

    swaps = {}
    for away in (4, 3, 5, 2, 6, 1, 7, 0):
        target = (z + away) % RING
        for t in range(2):
            sib_out[target, t] = partial(t, target, 1 - core).astype(BF16)
        c = remote(
            sib_out.at[target], sib_in.at[target], ss_send.at[away], ss_recv.at[away], sibling
        )
        c.start()
        swaps[away] = c

    def chip_sum(t, target):
        return partial(t, target, core) + sib_in[target, t].astype(F32)

    seen = set()
    hop_out = {}
    for left in (4, 3, 2, 1):
        for f, (t, way, hops) in enumerate(FLOWS):
            if left > hops:
                continue
            away = (way * left) % RING
            if away not in seen:
                seen.add(away)
                swaps[away].wait_recv()
            target = (z + away) % RING
            value = chip_sum(t, target)
            if left < hops:
                hop_out[f, left + 1].wait_recv()
                value += ring_in[f, left].astype(F32)
            ring_out[f, left - 1] = value.astype(BF16)
            c = remote(
                ring_out.at[f, left - 1], ring_in.at[f, left - 1],
                rs_send.at[f, left - 1], rs_recv.at[f, left - 1], up if way > 0 else down,
            )
            c.start()
            hop_out[f, left] = c
    swaps[0].wait_recv()
    for t, dst in enumerate((dk_out, dv_out)):
        value = chip_sum(t, z)
        for f, (tf, way, hops) in enumerate(FLOWS):
            if tf == t:
                hop_out[f, 1].wait_recv()
                value += ring_in[f, 0].astype(F32)
        dst[...] = value.astype(BF16)

    for h in range(2):
        dst = dq_out.at[:, pl.ds(pl.multiple_of((col * 2 + h) * HD, HD), HD)]
        pltpu.make_async_copy(dqs.at[h, pl.ds(mine, BLK), :], dst, dq_own.at[h]).wait()
        for dx, dy in MOVES:
            to = ((x + dx) % SIDE) * SIDE + (y + dy) % SIDE
            src = dqs.at[h, pl.ds(pl.multiple_of(to * BLK, BLK), BLK), :]
            into = dq_out.at[:, pl.ds(pl.multiple_of((to * 2 + h) * HD, HD), HD)]
            remote(src, into, dq_send.at[h, to], dq_recv.at[h, to], at_xy(dx, dy)).wait()
    for c in list(ring.values()) + list(side.values()) + exchange + list(swaps.values()) + list(hop_out.values()):
        c.wait_send()


def on_device(queries, grad_out, key_states, value_states, offsets, windows):
    rows, width = queries.shape[1:]
    anywhere = pl.BlockSpec(memory_space=pl.ANY)
    vmem = pl.BlockSpec(memory_space=pltpu.VMEM)
    smem = pl.BlockSpec(memory_space=pltpu.SMEM)
    dma = pltpu.SemaphoreType.DMA
    dq, dk, dv = pl.pallas_call(
        fused_kernel,
        out_shape=(
            jax.ShapeDtypeStruct((rows, width), BF16),
            jax.ShapeDtypeStruct(key_states.shape, BF16),
            jax.ShapeDtypeStruct(key_states.shape, BF16),
        ),
        in_specs=[smem, smem] + [anywhere] * 4,
        out_specs=(anywhere, vmem, vmem),
        scratch_shapes=[
            pltpu.VMEM((2, 2, PEERS * BLK, HD), BF16),
            pltpu.VMEM((2, 2, PAD, HD), BF16),
            pltpu.VMEM((2, HD, PAD), BF16),
            pltpu.VMEM((2, 2, PAD, HD), F32),
            pltpu.VMEM((SPAN, 2 * BLK), F32),
            pltpu.VMEM((SPAN, 2 * BLK), F32),
            pltpu.VMEM((TAIL, 2 * BLK), BF16),
            pltpu.VMEM((2, PEERS * BLK, HD), BF16),
            pltpu.VMEM((RING, 2, SHARD, HD), BF16),
            pltpu.VMEM((RING, 2, SHARD, HD), BF16),
            pltpu.VMEM((4, 4, SHARD, HD), BF16),
            pltpu.VMEM((4, 4, SHARD, HD), BF16),
            dma((2, 2, 15)), dma((2, 2, 15)), dma((3, 2)),
            dma((4, 4)), dma((4, 4)), dma((5, 4)), dma((5, 4)),
            dma((2, 16)), dma((2, 16)), dma((2,)),
            dma((8,)), dma((8,)), dma((4, 4)), dma((4, 4)),
        ],
        compiler_params=pltpu.CompilerParams(
            collective_id=0, has_side_effects=True, vmem_limit_bytes=56 << 20
        ),
    )(
        offsets, windows, queries.reshape(rows, width), grad_out.reshape(rows, width),
        key_states, value_states,
    )
    return dq.reshape(1, rows, width), dk, dv


def solution(mesh):
    in_specs = (
        P("depth", "seq", None),
        P("depth", "seq", None),
        P("depth", "seq"),
        P("depth", "seq"),
        P(),
        P(),
    )
    out_specs = (P("depth", "seq", None), P("depth", "seq"), P("depth", "seq"))
    return jax.shard_map(
        on_device, mesh=mesh, in_specs=in_specs, out_specs=out_specs, check_vma=False
    )
```

```python
import functools
import math

import jax
import jax.numpy as jnp
from jax import lax
from jax.experimental import pallas as pl
from jax.experimental.pallas import tpu as pltpu
from jax.sharding import PartitionSpec as P

HD = 128
WIN = 1024
BLK = 128
SIDE = 4
PEERS = SIDE * SIDE
RING = 8
SHARD = 512
TOTAL = 4096
PAD = TOTAL + WIN + BLK
SPAN = WIN + 3 * BLK + 16
TAIL = 1536
NEG = -1e30
SCALE = 1.0 / math.sqrt(HD)
SCALE2 = SCALE * math.log2(math.e)
F32 = jnp.float32
BF16 = jnp.bfloat16
MESH = pl.DeviceIdType.MESH

BLOCKS = (
    (0, 256, "a", "low"),
    (256, 384, "ab", "low"),
    (640, 384, "ab", "low"),
    (1024, 144, "ab", "high"),
    (1168, 112, "b", None),
    (1280, 144, "b", "high"),
)
COLS = {"a": (0, BLK), "b": (BLK, BLK), "ab": (0, 2 * BLK)}
MOVES = (
    (0, 1), (1, 0), (0, 3), (3, 0), (1, 1), (3, 3), (1, 3), (3, 1),
    (0, 2), (2, 0), (2, 1), (1, 2), (2, 3), (3, 2), (2, 2),
)
FLOWS = ((0, 1, 4), (1, -1, 4), (0, -1, 3), (1, 1, 3))
SUM_HOPS = {-1: 4, 1: 3}


def dot_t(a, b):
    return lax.dot_general(a, b, (((1,), (1,)), ((), ())), preferred_element_type=F32)


def dot(a, b):
    return jnp.dot(a, b, preferred_element_type=F32)


def fused_kernel(
    off_ref, win_ref, q_in, g_in, k_in, v_in,
    dq_out, dk_out, dv_out,
    qg, kv, kt, acc, s_scr, dp_scr, ds_scr, dqs, sib_out, sib_in, ring_out, ring_in,
    x_send, x_recv, own_sem, ag_send, ag_recv, sb_send, sb_recv, dq_send, dq_recv, dq_own,
    ss_send, ss_recv, rs_send, rs_recv,
):
    depth = lax.axis_index("depth")
    seq = lax.axis_index("seq")
    core = depth % 2
    z_lo = seq % 2
    col = seq // 2
    x = col // SIDE
    y = col % SIDE
    z = (depth // 2) * 2 + z_lo

    def at_xy(dx, dy):
        return (depth, (((x + dx) % SIDE) * SIDE + (y + dy) % SIDE) * 2 + z_lo)

    def at_z(to):
        return ((to // 2) * 2 + core, col * 2 + to % 2)

    up = at_z((z + 1) % RING)
    down = at_z((z + RING - 1) % RING)
    sibling = (depth + 1 - 2 * core, seq)

    barrier = pltpu.get_barrier_semaphore()
    partners = [at_xy(*m) for m in MOVES] + [up, down, sibling]
    for dev in partners:
        pl.semaphore_signal(barrier, inc=1, device_id=dev, device_id_type=MESH)
    pl.semaphore_wait(barrier, len(partners))

    def remote(src, dst, send, recv, dev):
        return pltpu.make_async_remote_copy(
            src_ref=src, dst_ref=dst, send_sem=send, recv_sem=recv, device_id=dev, device_id_type=MESH
        )

    def slot(t, origin, side):
        row = pl.multiple_of(WIN + ((origin // 2) * 2 + side) * SHARD, SHARD)
        return kv.at[t, origin % 2, pl.ds(row, SHARD), :]

    own_kv = (k_in, v_in)

    def along(way):
        return up if way > 0 else down

    def ring_copy(f, hop, src, dst):
        return remote(src, dst, ag_send.at[f, hop], ag_recv.at[f, hop], along(FLOWS[f][1]))

    def side_copy(f, hop, src, dst):
        return remote(src, dst, sb_send.at[f, hop], sb_recv.at[f, hop], sibling)

    def send_own():
        for f, (t, way, hops) in enumerate(FLOWS):
            ring_copy(f, 0, own_kv[t], slot(t, z, core)).start()
        for t in range(2):
            side_copy(4, t, own_kv[t], slot(t, z, core)).start()

    def turn(origin, side):
        row = pl.multiple_of(WIN + ((origin // 2) * 2 + side) * SHARD, SHARD)
        kt[origin % 2, :, pl.ds(row, SHARD)] = kv[0, origin % 2, pl.ds(row, SHARD), :].T

    def ring_step(h, r):
        far = (z + h) % 2
        away = 2 * r - far
        for f, (t, way, hops) in enumerate(FLOWS):
            origin = (z + 2 * RING - way * away) % RING
            here = slot(t, origin, core)

            @pl.when(away <= hops)
            def _():
                ring_copy(f, away - 1, here, here).wait_recv()

                @pl.when(away < hops)
                def _():
                    ring_copy(f, away, here, here).start()

                side_copy(f, away - 1, here, here).start()

        for f, (t, way, hops) in enumerate(FLOWS):
            if t == 0:
                origin = (z + 2 * RING - way * away) % RING

                @pl.when(away <= hops)
                def _():
                    turn(origin, core)

    def side_wait(h):
        far = (z + h) % 2

        @pl.when(far == 0)
        def _():
            for t in range(2):
                there = slot(t, z, 1 - core)
                side_copy(4, t, there, there).wait_recv()
            turn(z, 1 - core)

        for r in (1, 2):
            away = 2 * r - far
            for f, (t, way, hops) in enumerate(FLOWS):
                origin = (z + 2 * RING - way * away) % RING
                there = slot(t, origin, 1 - core)

                @pl.when(away <= hops)
                def _():
                    side_copy(f, away - 1, there, there).wait_recv()
                    if t == 0:
                        turn(origin, 1 - core)

    mine = pl.multiple_of(col * BLK, BLK)

    def cross(h):
        for i, (dx, dy) in enumerate(MOVES):
            for t, src in enumerate((q_in, g_in)):
                to = ((x + dx) % SIDE) * SIDE + (y + dy) % SIDE
                yield remote(
                    src.at[:, pl.ds(pl.multiple_of((to * 2 + h) * HD, HD), HD)],
                    qg.at[h, t, pl.ds(mine, BLK), :],
                    x_send.at[h, t, i],
                    x_recv.at[h, t, i],
                    at_xy(dx, dy),
                )

    local = []
    for t in range(2):
        local.append(pltpu.make_async_copy(own_kv[t], slot(t, z, core), own_sem.at[0, t]))
    for h in range(2):
        for t, src in enumerate((q_in, g_in)):
            local.append(
                pltpu.make_async_copy(
                    src.at[:, pl.ds(pl.multiple_of((col * 2 + h) * HD, HD), HD)],
                    qg.at[h, t, pl.ds(mine, BLK), :],
                    own_sem.at[1 + h, t],
                )
            )

    @pl.when(z_lo == 1)
    def _():
        send_own()

    for c in cross(1):
        c.start()
    for c in local:
        c.start()
    for h in range(2):
        for t in range(2):
            kv[t, h, pl.ds(0, WIN), :] = jnp.zeros((WIN, HD), BF16)
            kv[t, h, pl.ds(WIN + TOTAL, BLK), :] = jnp.zeros((BLK, HD), BF16)
        kt[h, :, pl.ds(0, WIN)] = jnp.zeros((HD, WIN), BF16)
        kt[h, :, pl.ds(WIN + TOTAL, BLK)] = jnp.zeros((HD, BLK), BF16)
    acc[...] = jnp.zeros_like(acc)
    ds_scr[...] = jnp.zeros_like(ds_scr)
    for c in local:
        c.wait()

    ring_step(1, 1)

    @pl.when(z_lo == 0)
    def _():
        send_own()

    turn(z, core)

    @pl.when(z_lo == 1)
    def _():
        ring_step(0, 1)

    for c in cross(1):
        c.wait_send()
    for c in cross(0):
        c.start()
    ring_step(1, 2)

    @pl.when(z_lo == 0)
    def _():
        ring_step(0, 1)

    side_wait(1)
    for c in cross(1):
        c.wait_recv()

    quarter = depth // 2

    def partial(t, target, side):
        row = pl.multiple_of(WIN + ((target // 2) * 2 + side) * SHARD, SHARD)
        value = acc[t, target % 2, pl.ds(row, SHARD), :]
        return value * SCALE if t == 0 else value

    def swap_copy(target):
        return remote(
            sib_out.at[target], sib_in.at[target], ss_send.at[target], ss_recv.at[target], sibling
        )

    def swap(h, ahead):
        target = ((quarter + ahead) % 4) * 2 + h
        for t in range(2):
            sib_out[target, t] = partial(t, target, 1 - core).astype(BF16)
        swap_copy(target).start()

    def chip_sum(t, target):
        return partial(t, target, core) + sib_in[target, t].astype(F32)

    def sum_copy(t, way, left):
        f = 2 * t + (1 if way > 0 else 0)
        return remote(
            ring_out.at[f, left - 1], ring_in.at[f, left - 1],
            rs_send.at[f, left - 1], rs_recv.at[f, left - 1], along(way),
        )

    def sum_round(h, far_round, way, near, add):
        left = (4 if far_round else 2) - near

        @pl.when((z + h) % 2 == near)
        def _():
            target = (z + RING + way * left) % RING
            swap_copy(target).wait_recv()
            for t in range(2):
                f = 2 * t + (1 if way > 0 else 0)
                value = chip_sum(t, target)
                if add:
                    sum_copy(t, way, left + 1).wait_recv()
                    value += ring_in[f, left].astype(F32)
                ring_out[f, left - 1] = value.astype(BF16)
                sum_copy(t, way, left).start()

    shift = off_ref[depth]
    span = win_ref[depth]
    lane = lax.broadcasted_iota(jnp.int32, (1, 2 * BLK), 1)
    place = lane + jnp.where(lane >= BLK, BLK, 0)
    last = place + WIN + shift

    def steps(n):
        def step(k):
            return pl.when(n == k)

        @pl.when(n == 5 - 2 * z_lo)
        def _():
            ring_step(0, 2)

        @step(5)
        def _():
            swap(1, 2)

        @step(7)
        def _():
            swap(1, 3)

        @step(8)
        def _():
            swap(1, 0)
            swap(1, 1)
            side_wait(0)
            for c in cross(0):
                c.wait_recv()

        @step(9)
        def _():
            sum_round(1, True, -1, 0, False)
            sum_round(1, True, 1, 1, False)

        @step(11)
        def _():
            sum_round(1, True, -1, 1, True)

        @step(12 + z_lo)
        def _():
            swap(0, 2)

        @step(12)
        def _():
            sum_round(1, False, 1, 0, True)

        @step(13)
        def _():
            sum_round(1, False, -1, 0, True)
            sum_round(0, True, -1, 0, False)

        @step(14 + z_lo)
        def _():
            swap(0, 3)

        @step(14)
        def _():
            sum_round(0, True, 1, 1, False)

        @step(15)
        def _():
            sum_round(1, False, 1, 1, True)
            sum_round(1, False, -1, 1, True)
            sum_round(0, True, -1, 1, True)

    def tile(n, carry):
        steps(n)
        h = 1 - n // 8
        u = (2 * quarter + 4 - z_lo + n) % 8
        base = pl.multiple_of((4 * u + z_lo) * BLK, BLK)
        low = jnp.maximum(last - span, WIN - 1 - base)
        high = jnp.minimum(last, TOTAL + WIN - 1 - base)
        rows_q = pl.multiple_of(u * 2 * BLK, 2 * BLK)
        q = qg[h, 0, pl.ds(rows_q, 2 * BLK), :]
        g = qg[h, 1, pl.ds(rows_q, 2 * BLK), :]

        def join(part, value, halves, op):
            c0, n0 = COLS[halves]
            if halves == "ab":
                return op(part, value)
            if halves == "a":
                return jnp.concatenate([op(part[:, :BLK], value), part[:, BLK:]], axis=1)
            return jnp.concatenate([part[:, :BLK], op(part[:, BLK:], value)], axis=1)

        top = jnp.full((1, 2 * BLK), NEG, F32)
        for k0, rows, halves, bound in BLOCKS:
            c0, cn = COLS[halves]
            at = pl.multiple_of(base + k0, 16)
            s = dot_t(kv[0, h, pl.ds(at, rows), :], q[c0 : c0 + cn])
            if bound is not None:
                key = lax.broadcasted_iota(jnp.int32, (rows, cn), 0)
                if bound == "low":
                    keep = key > low[:, c0 : c0 + cn] - k0
                else:
                    keep = key <= high[:, c0 : c0 + cn] - k0
                s = jnp.where(keep, s, NEG)
            s_scr[pl.ds(k0, rows), pl.ds(c0, cn)] = s
            top = join(top, jnp.max(s, axis=0, keepdims=True), halves, jnp.maximum)
        top = top * SCALE2
        sum_e = jnp.zeros((1, 2 * BLK), F32)
        sum_d = jnp.zeros((1, 2 * BLK), F32)
        for k0, rows, halves, bound in BLOCKS:
            c0, cn = COLS[halves]
            at = pl.multiple_of(base + k0, 16)
            dp = dot_t(kv[1, h, pl.ds(at, rows), :], g[c0 : c0 + cn])
            e = jnp.exp2(s_scr[pl.ds(k0, rows), pl.ds(c0, cn)] * SCALE2 - top[:, c0 : c0 + cn])
            sum_e = join(sum_e, jnp.sum(e, axis=0, keepdims=True), halves, jnp.add)
            sum_d = join(sum_d, jnp.sum(e * dp, axis=0, keepdims=True), halves, jnp.add)
            s_scr[pl.ds(k0, rows), pl.ds(c0, cn)] = e
            dp_scr[pl.ds(k0, rows), pl.ds(c0, cn)] = dp
        inv = 1.0 / sum_e
        rowdot = sum_d * inv
        for k0, rows, halves, bound in BLOCKS:
            c0, cn = COLS[halves]
            at = pl.multiple_of(base + k0, 16)
            p = s_scr[pl.ds(k0, rows), pl.ds(c0, cn)] * inv[:, c0 : c0 + cn]
            ds = p * (dp_scr[pl.ds(k0, rows), pl.ds(c0, cn)] - rowdot[:, c0 : c0 + cn])
            ds = ds.astype(BF16)
            ds_scr[pl.ds(k0, rows), pl.ds(c0, cn)] = ds
            acc[1, h, pl.ds(at, rows), :] += dot(p.astype(BF16), g[c0 : c0 + cn])
            acc[0, h, pl.ds(at, rows), :] += dot(ds, q[c0 : c0 + cn])
        dqt = dot(kt[h, :, pl.ds(base, TAIL)], ds_scr[...])
        dqs[h, pl.ds(rows_q, 2 * BLK), :] = (dqt.T * SCALE).astype(BF16)

        for half in range(2):
            to = 2 * u + half
            src = dqs.at[h, pl.ds(pl.multiple_of(to * BLK, BLK), BLK), :]
            dst = dq_out.at[:, pl.ds(pl.multiple_of((col * 2 + h) * HD, HD), HD)]

            @pl.when(to != col)
            def _():
                remote(src, dst, dq_send.at[h, to], dq_recv.at[h, col], (depth, to * 2 + z_lo)).start()

            @pl.when(to == col)
            def _():
                pltpu.make_async_copy(src, dst, dq_own.at[h]).start()

        return carry

    lax.fori_loop(0, 16, tile, 0)

    swap(0, 1)
    swap(0, 0)
    sum_round(0, False, -1, 0, True)
    sum_round(0, False, 1, 0, True)
    sum_round(0, False, -1, 1, True)
    sum_round(0, False, 1, 1, True)
    swap_copy(z).wait_recv()
    for t, dst in enumerate((dk_out, dv_out)):
        value = chip_sum(t, z)
        for way in (-1, 1):
            sum_copy(t, way, 1).wait_recv()
            value += ring_in[2 * t + (1 if way > 0 else 0), 0].astype(F32)
        dst[...] = value.astype(BF16)

    for h in range(2):
        dst = dq_out.at[:, pl.ds(pl.multiple_of((col * 2 + h) * HD, HD), HD)]
        pltpu.make_async_copy(dqs.at[h, pl.ds(mine, BLK), :], dst, dq_own.at[h]).wait()
        for dx, dy in MOVES:
            to = ((x + dx) % SIDE) * SIDE + (y + dy) % SIDE
            src = dqs.at[h, pl.ds(pl.multiple_of(to * BLK, BLK), BLK), :]
            into = dq_out.at[:, pl.ds(pl.multiple_of((to * 2 + h) * HD, HD), HD)]
            remote(src, into, dq_send.at[h, to], dq_recv.at[h, to], at_xy(dx, dy)).wait()
    for f, (t, way, hops) in enumerate(FLOWS):
        for hop in range(hops):
            here = slot(t, z, core)
            ring_copy(f, hop, here, here).wait_send()
            side_copy(f, hop, here, here).wait_send()
    for t in range(2):
        here = slot(t, z, core)
        side_copy(4, t, here, here).wait_send()
    for c in cross(0):
        c.wait_send()
    for target in range(RING):
        swap_copy(target).wait_send()
    for way, hops in SUM_HOPS.items():
        for t in range(2):
            for left in range(1, hops + 1):
                sum_copy(t, way, left).wait_send()


def on_device(queries, grad_out, key_states, value_states, offsets, windows):
    rows, width = queries.shape[1:]
    anywhere = pl.BlockSpec(memory_space=pl.ANY)
    vmem = pl.BlockSpec(memory_space=pltpu.VMEM)
    smem = pl.BlockSpec(memory_space=pltpu.SMEM)
    dma = pltpu.SemaphoreType.DMA
    dq, dk, dv = pl.pallas_call(
        fused_kernel,
        out_shape=(
            jax.ShapeDtypeStruct((rows, width), BF16),
            jax.ShapeDtypeStruct(key_states.shape, BF16),
            jax.ShapeDtypeStruct(key_states.shape, BF16),
        ),
        in_specs=[smem, smem] + [anywhere] * 4,
        out_specs=(anywhere, vmem, vmem),
        scratch_shapes=[
            pltpu.VMEM((2, 2, PEERS * BLK, HD), BF16),
            pltpu.VMEM((2, 2, PAD, HD), BF16),
            pltpu.VMEM((2, HD, PAD), BF16),
            pltpu.VMEM((2, 2, PAD, HD), F32),
            pltpu.VMEM((SPAN, 2 * BLK), F32),
            pltpu.VMEM((SPAN, 2 * BLK), F32),
            pltpu.VMEM((TAIL, 2 * BLK), BF16),
            pltpu.VMEM((2, PEERS * BLK, HD), BF16),
            pltpu.VMEM((RING, 2, SHARD, HD), BF16),
            pltpu.VMEM((RING, 2, SHARD, HD), BF16),
            pltpu.VMEM((4, 4, SHARD, HD), BF16),
            pltpu.VMEM((4, 4, SHARD, HD), BF16),
            dma((2, 2, 15)), dma((2, 2, 15)), dma((3, 2)),
            dma((4, 4)), dma((4, 4)), dma((5, 4)), dma((5, 4)),
            dma((2, 16)), dma((2, 16)), dma((2,)),
            dma((8,)), dma((8,)), dma((4, 4)), dma((4, 4)),
        ],
        compiler_params=pltpu.CompilerParams(
            collective_id=0, has_side_effects=True, vmem_limit_bytes=56 << 20
        ),
    )(
        offsets, windows, queries.reshape(rows, width), grad_out.reshape(rows, width),
        key_states, value_states,
    )
    return dq.reshape(1, rows, width), dk, dv


def solution(mesh):
    in_specs = (
        P("depth", "seq", None),
        P("depth", "seq", None),
        P("depth", "seq"),
        P("depth", "seq"),
        P(),
        P(),
    )
    out_specs = (P("depth", "seq", None), P("depth", "seq"), P("depth", "seq"))
    return jax.shard_map(
        on_device, mesh=mesh, in_specs=in_specs, out_specs=out_specs, check_vma=False
    )
```

```python
import functools
import math

import jax
import jax.numpy as jnp
from jax import lax
from jax.experimental import pallas as pl
from jax.experimental.pallas import tpu as pltpu
from jax.sharding import PartitionSpec as P

HD = 128
WIN = 1024
BLK = 128
SIDE = 4
PEERS = SIDE * SIDE
RING = 8
SHARD = 512
TOTAL = 4096
PAD = TOTAL + WIN + BLK
SPAN = WIN + 3 * BLK + 16
TAIL = 1536
NEG = -1e30
SCALE = 1.0 / math.sqrt(HD)
SCALE2 = SCALE * math.log2(math.e)
F32 = jnp.float32
BF16 = jnp.bfloat16
MESH = pl.DeviceIdType.MESH

BLOCKS = (
    (0, 256, "a", "low"),
    (256, 384, "ab", "low"),
    (640, 384, "ab", "low"),
    (1024, 144, "ab", "high"),
    (1168, 112, "b", None),
    (1280, 144, "b", "high"),
)
COLS = {"a": (0, BLK), "b": (BLK, BLK), "ab": (0, 2 * BLK)}
MOVES = (
    (0, 1), (1, 0), (0, 3), (3, 0), (1, 1), (3, 3), (1, 3), (3, 1),
    (0, 2), (2, 0), (2, 1), (1, 2), (2, 3), (3, 2), (2, 2),
)
FLOWS = ((0, 1, 4), (1, -1, 4), (0, -1, 3), (1, 1, 3))
HOPS = {(t, way): hops for t, way, hops in FLOWS}


def dot_t(a, b):
    return lax.dot_general(a, b, (((1,), (1,)), ((), ())), preferred_element_type=F32)


def dot(a, b):
    return jnp.dot(a, b, preferred_element_type=F32)


def fused_kernel(
    off_ref, win_ref, q_in, g_in, k_in, v_in,
    dq_out, dk_out, dv_out,
    qg, kv, kt, acc, s_scr, dp_scr, ds_scr, dqs, sib_out, sib_in, ring_out, ring_in,
    x_send, x_recv, own_sem, ag_send, ag_recv, sb_send, sb_recv, dq_send, dq_recv, dq_own,
    ss_send, ss_recv, rs_send, rs_recv,
):
    depth = lax.axis_index("depth")
    seq = lax.axis_index("seq")
    core = depth % 2
    z_lo = seq % 2
    col = seq // 2
    x = col // SIDE
    y = col % SIDE
    z = (depth // 2) * 2 + z_lo

    def at_xy(dx, dy):
        return (depth, (((x + dx) % SIDE) * SIDE + (y + dy) % SIDE) * 2 + z_lo)

    def at_z(to):
        return ((to // 2) * 2 + core, col * 2 + to % 2)

    up = at_z((z + 1) % RING)
    down = at_z((z + RING - 1) % RING)
    sibling = (depth + 1 - 2 * core, seq)

    barrier = pltpu.get_barrier_semaphore()
    partners = [at_xy(*m) for m in MOVES] + [up, down, sibling]
    for dev in partners:
        pl.semaphore_signal(barrier, inc=1, device_id=dev, device_id_type=MESH)
    pl.semaphore_wait(barrier, len(partners))

    def remote(src, dst, send, recv, dev):
        return pltpu.make_async_remote_copy(
            src_ref=src, dst_ref=dst, send_sem=send, recv_sem=recv, device_id=dev, device_id_type=MESH
        )

    def slot(t, origin, side):
        row = pl.multiple_of(WIN + ((origin // 2) * 2 + side) * SHARD, SHARD)
        return kv.at[t, origin % 2, pl.ds(row, SHARD), :]

    own_kv = (k_in, v_in)

    def along(way):
        return up if way > 0 else down

    def ring_copy(f, hop, src, dst):
        return remote(src, dst, ag_send.at[f, hop], ag_recv.at[f, hop], along(FLOWS[f][1]))

    def side_copy(f, hop, src, dst):
        return remote(src, dst, sb_send.at[f, hop], sb_recv.at[f, hop], sibling)

    def send_own():
        for f, (t, way, hops) in enumerate(FLOWS):
            ring_copy(f, 0, own_kv[t], slot(t, z, core)).start()
        for t in range(2):
            side_copy(4, t, own_kv[t], slot(t, z, core)).start()

    def turn(origin, side):
        row = pl.multiple_of(WIN + ((origin // 2) * 2 + side) * SHARD, SHARD)
        kt[origin % 2, :, pl.ds(row, SHARD)] = kv[0, origin % 2, pl.ds(row, SHARD), :].T

    def origin_of(way, away):
        return (z + RING - way * away) % RING

    def ring_step(away):
        flows = [(f, t, way, hops) for f, (t, way, hops) in enumerate(FLOWS) if away <= hops]
        for f, t, way, hops in flows:
            here = slot(t, origin_of(way, away), core)
            ring_copy(f, away - 1, here, here).wait_recv()
            if away < hops:
                ring_copy(f, away, here, here).start()
            side_copy(f, away - 1, here, here).start()
        for f, t, way, hops in flows:
            if t == 0:
                turn(origin_of(way, away), core)

    def side_wait(away):
        if away == 0:
            for t in range(2):
                there = slot(t, z, 1 - core)
                side_copy(4, t, there, there).wait_recv()
            turn(z, 1 - core)
            return
        for f, (t, way, hops) in enumerate(FLOWS):
            if away <= hops:
                there = slot(t, origin_of(way, away), 1 - core)
                side_copy(f, away - 1, there, there).wait_recv()
                if t == 0:
                    turn(origin_of(way, away), 1 - core)

    heads = (1 - z_lo, z_lo)

    mine = pl.multiple_of(col * BLK, BLK)

    def cross(order):
        h = heads[order]
        for i, (dx, dy) in enumerate(MOVES):
            for t, src in enumerate((q_in, g_in)):
                to = ((x + dx) % SIDE) * SIDE + (y + dy) % SIDE
                yield remote(
                    src.at[:, pl.ds(pl.multiple_of((to * 2 + h) * HD, HD), HD)],
                    qg.at[order, t, pl.ds(mine, BLK), :],
                    x_send.at[order, t, i],
                    x_recv.at[order, t, i],
                    at_xy(dx, dy),
                )

    local = []
    for t in range(2):
        local.append(pltpu.make_async_copy(own_kv[t], slot(t, z, core), own_sem.at[0, t]))
    for order in range(2):
        for t, src in enumerate((q_in, g_in)):
            local.append(
                pltpu.make_async_copy(
                    src.at[:, pl.ds(pl.multiple_of((col * 2 + heads[order]) * HD, HD), HD)],
                    qg.at[order, t, pl.ds(mine, BLK), :],
                    own_sem.at[1 + order, t],
                )
            )

    send_own()
    for order in range(2):
        for c in cross(order):
            c.start()
    for c in local:
        c.start()
    for h in range(2):
        for t in range(2):
            kv[t, h, pl.ds(0, WIN), :] = jnp.zeros((WIN, HD), BF16)
            kv[t, h, pl.ds(WIN + TOTAL, BLK), :] = jnp.zeros((BLK, HD), BF16)
        kt[h, :, pl.ds(0, WIN)] = jnp.zeros((HD, WIN), BF16)
        kt[h, :, pl.ds(WIN + TOTAL, BLK)] = jnp.zeros((HD, BLK), BF16)
    acc[...] = jnp.zeros_like(acc)
    ds_scr[...] = jnp.zeros_like(ds_scr)
    for c in local:
        c.wait()

    turn(z, core)
    ring_step(1)
    ring_step(2)
    ring_step(3)
    side_wait(1)
    side_wait(3)
    for c in cross(0):
        c.wait_recv()

    quarter = depth // 2

    def partial(t, target, side):
        row = pl.multiple_of(WIN + ((target // 2) * 2 + side) * SHARD, SHARD)
        value = acc[t, target % 2, pl.ds(row, SHARD), :]
        return value * SCALE if t == 0 else value

    def swap_copy(target):
        return remote(
            sib_out.at[target], sib_in.at[target], ss_send.at[target], ss_recv.at[target], sibling
        )

    def swap(away):
        target = (z + away) % RING
        for t in range(2):
            sib_out[target, t] = partial(t, target, 1 - core).astype(BF16)
        swap_copy(target).start()

    def chip_sum(t, target):
        return partial(t, target, core) + sib_in[target, t].astype(F32)

    def sum_copy(t, way, left):
        f = 2 * t + (1 if way > 0 else 0)
        return remote(
            ring_out.at[f, left - 1], ring_in.at[f, left - 1],
            rs_send.at[f, left - 1], rs_recv.at[f, left - 1], along(way),
        )

    def sum_round(t, way, left):
        value = chip_sum(t, (z + RING + way * left) % RING)
        if left < HOPS[t, way]:
            sum_copy(t, way, left + 1).wait_recv()
            value += ring_in[2 * t + (1 if way > 0 else 0), left].astype(F32)
        ring_out[2 * t + (1 if way > 0 else 0), left - 1] = value.astype(BF16)
        sum_copy(t, way, left).start()

    def swap_wait(away):
        swap_copy((z + away) % RING).wait_recv()

    shift = off_ref[depth]
    span = win_ref[depth]
    lane = lax.broadcasted_iota(jnp.int32, (1, 2 * BLK), 1)
    place = lane + jnp.where(lane >= BLK, BLK, 0)
    last = place + WIN + shift

    def steps(n):
        def step(k):
            return pl.when(n == k)

        @step(4)
        def _():
            ring_step(4)

        @step(8)
        def _():
            side_wait(0)
            side_wait(2)
            side_wait(4)
            for c in cross(1):
                c.wait_recv()
            for away in (3, 5, 1, 7):
                swap(away)

        @step(10)
        def _():
            for away in (3, 5, 1, 7):
                swap_wait(away)
            sum_round(0, -1, 3)
            sum_round(1, 1, 3)

        @step(12 + z_lo)
        def _():
            swap(4)

        @step(13 + z_lo)
        def _():
            swap_wait(4)
            sum_round(0, 1, 4)
            sum_round(1, -1, 4)

        @step(14 + z_lo)
        def _():
            swap(6)

        @step(15)
        def _():
            sum_round(0, 1, 3)
            sum_round(1, -1, 3)

    def tile(n, carry):
        steps(n)
        order = n // 8
        h = jnp.where(order == 0, heads[0], heads[1])
        u = (2 * quarter + 4 - z_lo + n) % 8
        base = pl.multiple_of((4 * u + z_lo) * BLK, BLK)
        low = jnp.maximum(last - span, WIN - 1 - base)
        high = jnp.minimum(last, TOTAL + WIN - 1 - base)
        rows_q = pl.multiple_of(u * 2 * BLK, 2 * BLK)
        q = qg[order, 0, pl.ds(rows_q, 2 * BLK), :]
        g = qg[order, 1, pl.ds(rows_q, 2 * BLK), :]

        def join(part, value, halves, op):
            c0, n0 = COLS[halves]
            if halves == "ab":
                return op(part, value)
            if halves == "a":
                return jnp.concatenate([op(part[:, :BLK], value), part[:, BLK:]], axis=1)
            return jnp.concatenate([part[:, :BLK], op(part[:, BLK:], value)], axis=1)

        top = jnp.full((1, 2 * BLK), NEG, F32)
        for k0, rows, halves, bound in BLOCKS:
            c0, cn = COLS[halves]
            at = pl.multiple_of(base + k0, 16)
            s = dot_t(kv[0, h, pl.ds(at, rows), :], q[c0 : c0 + cn])
            if bound is not None:
                key = lax.broadcasted_iota(jnp.int32, (rows, cn), 0)
                if bound == "low":
                    keep = key > low[:, c0 : c0 + cn] - k0
                else:
                    keep = key <= high[:, c0 : c0 + cn] - k0
                s = jnp.where(keep, s, NEG)
            s_scr[pl.ds(k0, rows), pl.ds(c0, cn)] = s
            top = join(top, jnp.max(s, axis=0, keepdims=True), halves, jnp.maximum)
        top = top * SCALE2
        sum_e = jnp.zeros((1, 2 * BLK), F32)
        sum_d = jnp.zeros((1, 2 * BLK), F32)
        for k0, rows, halves, bound in BLOCKS:
            c0, cn = COLS[halves]
            at = pl.multiple_of(base + k0, 16)
            dp = dot_t(kv[1, h, pl.ds(at, rows), :], g[c0 : c0 + cn])
            e = jnp.exp2(s_scr[pl.ds(k0, rows), pl.ds(c0, cn)] * SCALE2 - top[:, c0 : c0 + cn])
            sum_e = join(sum_e, jnp.sum(e, axis=0, keepdims=True), halves, jnp.add)
            sum_d = join(sum_d, jnp.sum(e * dp, axis=0, keepdims=True), halves, jnp.add)
            s_scr[pl.ds(k0, rows), pl.ds(c0, cn)] = e
            dp_scr[pl.ds(k0, rows), pl.ds(c0, cn)] = dp
        inv = 1.0 / sum_e
        rowdot = sum_d * inv
        for k0, rows, halves, bound in BLOCKS:
            c0, cn = COLS[halves]
            at = pl.multiple_of(base + k0, 16)
            p = s_scr[pl.ds(k0, rows), pl.ds(c0, cn)] * inv[:, c0 : c0 + cn]
            ds = p * (dp_scr[pl.ds(k0, rows), pl.ds(c0, cn)] - rowdot[:, c0 : c0 + cn])
            ds = ds.astype(BF16)
            ds_scr[pl.ds(k0, rows), pl.ds(c0, cn)] = ds
            acc[1, h, pl.ds(at, rows), :] += dot(p.astype(BF16), g[c0 : c0 + cn])
            acc[0, h, pl.ds(at, rows), :] += dot(ds, q[c0 : c0 + cn])
        dqt = dot(kt[h, :, pl.ds(base, TAIL)], ds_scr[...])
        dqs[h, pl.ds(rows_q, 2 * BLK), :] = (dqt.T * SCALE).astype(BF16)

        for half in range(2):
            to = 2 * u + half
            src = dqs.at[h, pl.ds(pl.multiple_of(to * BLK, BLK), BLK), :]
            dst = dq_out.at[:, pl.ds(pl.multiple_of((col * 2 + h) * HD, HD), HD)]

            @pl.when(to != col)
            def _():
                remote(src, dst, dq_send.at[h, to], dq_recv.at[h, col], (depth, to * 2 + z_lo)).start()

            @pl.when(to == col)
            def _():
                pltpu.make_async_copy(src, dst, dq_own.at[h]).start()

        return carry

    lax.fori_loop(0, 16, tile, 0)

    swap(2)
    swap(0)
    swap_wait(6)
    sum_round(0, -1, 2)
    sum_round(1, -1, 2)
    swap_wait(2)
    sum_round(1, 1, 2)
    sum_round(0, 1, 2)
    for t in range(2):
        sum_round(t, -1, 1)
    for t in (1, 0):
        sum_round(t, 1, 1)
    swap_copy(z).wait_recv()
    for t, dst in enumerate((dk_out, dv_out)):
        value = chip_sum(t, z)
        for way in (-1, 1):
            sum_copy(t, way, 1).wait_recv()
            value += ring_in[2 * t + (1 if way > 0 else 0), 0].astype(F32)
        dst[...] = value.astype(BF16)

    for h in range(2):
        dst = dq_out.at[:, pl.ds(pl.multiple_of((col * 2 + h) * HD, HD), HD)]
        pltpu.make_async_copy(dqs.at[h, pl.ds(mine, BLK), :], dst, dq_own.at[h]).wait()
        for dx, dy in MOVES:
            to = ((x + dx) % SIDE) * SIDE + (y + dy) % SIDE
            src = dqs.at[h, pl.ds(pl.multiple_of(to * BLK, BLK), BLK), :]
            into = dq_out.at[:, pl.ds(pl.multiple_of((to * 2 + h) * HD, HD), HD)]
            remote(src, into, dq_send.at[h, to], dq_recv.at[h, to], at_xy(dx, dy)).wait()
    for f, (t, way, hops) in enumerate(FLOWS):
        for hop in range(hops):
            here = slot(t, z, core)
            ring_copy(f, hop, here, here).wait_send()
            side_copy(f, hop, here, here).wait_send()
    for t in range(2):
        here = slot(t, z, core)
        side_copy(4, t, here, here).wait_send()
    for order in range(2):
        for c in cross(order):
            c.wait_send()
    for target in range(RING):
        swap_copy(target).wait_send()
    for t, way, hops in FLOWS:
        for left in range(1, hops + 1):
            sum_copy(t, way, left).wait_send()


def on_device(queries, grad_out, key_states, value_states, offsets, windows):
    rows, width = queries.shape[1:]
    anywhere = pl.BlockSpec(memory_space=pl.ANY)
    vmem = pl.BlockSpec(memory_space=pltpu.VMEM)
    smem = pl.BlockSpec(memory_space=pltpu.SMEM)
    dma = pltpu.SemaphoreType.DMA
    dq, dk, dv = pl.pallas_call(
        fused_kernel,
        out_shape=(
            jax.ShapeDtypeStruct((rows, width), BF16),
            jax.ShapeDtypeStruct(key_states.shape, BF16),
            jax.ShapeDtypeStruct(key_states.shape, BF16),
        ),
        in_specs=[smem, smem] + [anywhere] * 4,
        out_specs=(anywhere, vmem, vmem),
        scratch_shapes=[
            pltpu.VMEM((2, 2, PEERS * BLK, HD), BF16),
            pltpu.VMEM((2, 2, PAD, HD), BF16),
            pltpu.VMEM((2, HD, PAD), BF16),
            pltpu.VMEM((2, 2, PAD, HD), F32),
            pltpu.VMEM((SPAN, 2 * BLK), F32),
            pltpu.VMEM((SPAN, 2 * BLK), F32),
            pltpu.VMEM((TAIL, 2 * BLK), BF16),
            pltpu.VMEM((2, PEERS * BLK, HD), BF16),
            pltpu.VMEM((RING, 2, SHARD, HD), BF16),
            pltpu.VMEM((RING, 2, SHARD, HD), BF16),
            pltpu.VMEM((4, 4, SHARD, HD), BF16),
            pltpu.VMEM((4, 4, SHARD, HD), BF16),
            dma((2, 2, 15)), dma((2, 2, 15)), dma((3, 2)),
            dma((4, 4)), dma((4, 4)), dma((5, 4)), dma((5, 4)),
            dma((2, 16)), dma((2, 16)), dma((2,)),
            dma((8,)), dma((8,)), dma((4, 4)), dma((4, 4)),
        ],
        compiler_params=pltpu.CompilerParams(
            collective_id=0, has_side_effects=True, vmem_limit_bytes=56 << 20
        ),
    )(
        offsets, windows, queries.reshape(rows, width), grad_out.reshape(rows, width),
        key_states, value_states,
    )
    return dq.reshape(1, rows, width), dk, dv


def solution(mesh):
    in_specs = (
        P("depth", "seq", None),
        P("depth", "seq", None),
        P("depth", "seq"),
        P("depth", "seq"),
        P(),
        P(),
    )
    out_specs = (P("depth", "seq", None), P("depth", "seq"), P("depth", "seq"))
    return jax.shard_map(
        on_device, mesh=mesh, in_specs=in_specs, out_specs=out_specs, check_vma=False
    )
```

```python
import functools
import math

import jax
import jax.numpy as jnp
from jax import lax
from jax.experimental import pallas as pl
from jax.experimental.pallas import tpu as pltpu
from jax.sharding import PartitionSpec as P

HD = 128
WIN = 1024
BLK = 128
SIDE = 4
PEERS = SIDE * SIDE
RING = 8
SHARD = 512
TOTAL = 4096
PAD = TOTAL + WIN + BLK
SPAN = WIN + 3 * BLK + 16
TAIL = 1536
NEG = -1e30
SCALE = 1.0 / math.sqrt(HD)
SCALE2 = SCALE * math.log2(math.e)
F32 = jnp.float32
BF16 = jnp.bfloat16
MESH = pl.DeviceIdType.MESH

BLOCKS = (
    (0, 256, "a", "low"),
    (256, 384, "ab", "low"),
    (640, 384, "ab", "low"),
    (1024, 144, "ab", "high"),
    (1168, 112, "b", None),
    (1280, 144, "b", "high"),
)
COLS = {"a": (0, BLK), "b": (BLK, BLK), "ab": (0, 2 * BLK)}
MOVES = (
    (0, 1), (1, 0), (0, 3), (3, 0), (1, 1), (3, 3), (1, 3), (3, 1),
    (0, 2), (2, 0), (2, 1), (1, 2), (2, 3), (3, 2), (2, 2),
)
FLOWS = ((0, 1, 4), (1, -1, 4), (0, -1, 3), (1, 1, 3))
HOPS = {(t, way): hops for t, way, hops in FLOWS}


def dot_t(a, b):
    return lax.dot_general(a, b, (((1,), (1,)), ((), ())), preferred_element_type=F32)


def dot(a, b):
    return jnp.dot(a, b, preferred_element_type=F32)


def fused_kernel(
    off_ref, win_ref, q_in, g_in, k_in, v_in,
    dq_out, dk_out, dv_out,
    qg, kv, kt, acc, s_scr, s_scr2, dp_scr, ds_scr, dqs, sib_out, sib_in, ring_out, ring_in,
    x_send, x_recv, own_sem, ag_send, ag_recv, sb_send, sb_recv, dq_send, dq_recv, dq_own,
    ss_send, ss_recv, rs_send, rs_recv,
):
    depth = lax.axis_index("depth")
    seq = lax.axis_index("seq")
    core = depth % 2
    z_lo = seq % 2
    col = seq // 2
    x = col // SIDE
    y = col % SIDE
    z = (depth // 2) * 2 + z_lo

    def at_xy(dx, dy):
        return (depth, (((x + dx) % SIDE) * SIDE + (y + dy) % SIDE) * 2 + z_lo)

    def at_z(to):
        return ((to // 2) * 2 + core, col * 2 + to % 2)

    up = at_z((z + 1) % RING)
    down = at_z((z + RING - 1) % RING)
    sibling = (depth + 1 - 2 * core, seq)

    barrier = pltpu.get_barrier_semaphore()
    partners = [at_xy(*m) for m in MOVES] + [up, down, sibling]
    for dev in partners:
        pl.semaphore_signal(barrier, inc=1, device_id=dev, device_id_type=MESH)
    pl.semaphore_wait(barrier, len(partners))

    def remote(src, dst, send, recv, dev):
        return pltpu.make_async_remote_copy(
            src_ref=src, dst_ref=dst, send_sem=send, recv_sem=recv, device_id=dev, device_id_type=MESH
        )

    def slot(t, origin, side):
        row = pl.multiple_of(WIN + ((origin // 2) * 2 + side) * SHARD, SHARD)
        return kv.at[t, origin % 2, pl.ds(row, SHARD), :]

    own_kv = (k_in, v_in)

    def along(way):
        return up if way > 0 else down

    def ring_copy(f, hop, src, dst):
        return remote(src, dst, ag_send.at[f, hop], ag_recv.at[f, hop], along(FLOWS[f][1]))

    def side_copy(f, hop, src, dst):
        return remote(src, dst, sb_send.at[f, hop], sb_recv.at[f, hop], sibling)

    def send_own():
        for f, (t, way, hops) in enumerate(FLOWS):
            ring_copy(f, 0, own_kv[t], slot(t, z, core)).start()
        for t in range(2):
            side_copy(4, t, own_kv[t], slot(t, z, core)).start()

    def turn(origin, side):
        row = pl.multiple_of(WIN + ((origin // 2) * 2 + side) * SHARD, SHARD)
        kt[origin % 2, :, pl.ds(row, SHARD)] = kv[0, origin % 2, pl.ds(row, SHARD), :].T

    def origin_of(way, away):
        return (z + RING - way * away) % RING

    def ring_step(away):
        flows = [(f, t, way, hops) for f, (t, way, hops) in enumerate(FLOWS) if away <= hops]
        for f, t, way, hops in flows:
            here = slot(t, origin_of(way, away), core)
            ring_copy(f, away - 1, here, here).wait_recv()
            if away < hops:
                ring_copy(f, away, here, here).start()
            side_copy(f, away - 1, here, here).start()
        for f, t, way, hops in flows:
            if t == 0:
                turn(origin_of(way, away), core)

    def side_wait(away):
        if away == 0:
            for t in range(2):
                there = slot(t, z, 1 - core)
                side_copy(4, t, there, there).wait_recv()
            turn(z, 1 - core)
            return
        for f, (t, way, hops) in enumerate(FLOWS):
            if away <= hops:
                there = slot(t, origin_of(way, away), 1 - core)
                side_copy(f, away - 1, there, there).wait_recv()
                if t == 0:
                    turn(origin_of(way, away), 1 - core)

    heads = (z_lo, 1 - z_lo)

    mine = pl.multiple_of(col * BLK, BLK)

    def cross(order):
        h = heads[order]
        for i, (dx, dy) in enumerate(MOVES):
            for t, src in enumerate((q_in, g_in)):
                to = ((x + dx) % SIDE) * SIDE + (y + dy) % SIDE
                yield remote(
                    src.at[:, pl.ds(pl.multiple_of((to * 2 + h) * HD, HD), HD)],
                    qg.at[order, t, pl.ds(mine, BLK), :],
                    x_send.at[order, t, i],
                    x_recv.at[order, t, i],
                    at_xy(dx, dy),
                )

    local = []
    for t in range(2):
        local.append(pltpu.make_async_copy(own_kv[t], slot(t, z, core), own_sem.at[0, t]))
    for order in range(2):
        for t, src in enumerate((q_in, g_in)):
            local.append(
                pltpu.make_async_copy(
                    src.at[:, pl.ds(pl.multiple_of((col * 2 + heads[order]) * HD, HD), HD)],
                    qg.at[order, t, pl.ds(mine, BLK), :],
                    own_sem.at[1 + order, t],
                )
            )

    send_own()
    for c in local:
        c.start()
    for order in range(2):
        for c in cross(order):
            c.start()
    for h in range(2):
        for t in range(2):
            kv[t, h, pl.ds(0, WIN), :] = jnp.zeros((WIN, HD), BF16)
            kv[t, h, pl.ds(WIN + TOTAL, BLK), :] = jnp.zeros((BLK, HD), BF16)
        kt[h, :, pl.ds(0, WIN)] = jnp.zeros((HD, WIN), BF16)
        kt[h, :, pl.ds(WIN + TOTAL, BLK)] = jnp.zeros((HD, BLK), BF16)
    acc[...] = jnp.zeros_like(acc)
    ds_scr[...] = jnp.zeros_like(ds_scr)
    local[0].wait()
    turn(z, core)
    ring_step(1)
    ring_step(2)
    side_wait(0)
    side_wait(2)
    for c in local[1:]:
        c.wait()
    for c in cross(0):
        c.wait_recv()

    quarter = depth // 2

    def partial(t, target, side):
        row = pl.multiple_of(WIN + ((target // 2) * 2 + side) * SHARD, SHARD)
        value = acc[t, target % 2, pl.ds(row, SHARD), :]
        return value * SCALE if t == 0 else value

    def swap_copy(target):
        return remote(
            sib_out.at[target], sib_in.at[target], ss_send.at[target], ss_recv.at[target], sibling
        )

    def swap(away):
        target = (z + away) % RING
        for t in range(2):
            sib_out[target, t] = partial(t, target, 1 - core).astype(BF16)
        swap_copy(target).start()

    def chip_sum(t, target):
        return partial(t, target, core) + sib_in[target, t].astype(F32)

    def sum_copy(t, way, left):
        f = 2 * t + (1 if way > 0 else 0)
        return remote(
            ring_out.at[f, left - 1], ring_in.at[f, left - 1],
            rs_send.at[f, left - 1], rs_recv.at[f, left - 1], along(way),
        )

    def sum_round(t, way, left):
        value = chip_sum(t, (z + RING + way * left) % RING)
        if left < HOPS[t, way]:
            sum_copy(t, way, left + 1).wait_recv()
            value += ring_in[2 * t + (1 if way > 0 else 0), left].astype(F32)
        ring_out[2 * t + (1 if way > 0 else 0), left - 1] = value.astype(BF16)
        sum_copy(t, way, left).start()

    def swap_wait(away):
        swap_copy((z + away) % RING).wait_recv()

    shift = off_ref[depth]
    span = win_ref[depth]
    lane = lax.broadcasted_iota(jnp.int32, (1, 2 * BLK), 1)
    place = lane + jnp.where(lane >= BLK, BLK, 0)
    last = place + WIN + shift

    def tile_of(n):
        order = n // 8
        h = jnp.where(order == 0, heads[0], heads[1])
        return order, h, (2 * quarter + n + order * (2 + z_lo)) % 8

    def send_dq(group, k):
        m = (k + col) % 2
        order, h, u = tile_of(group)
        to = 2 * u + m
        src = dqs.at[h, pl.ds(pl.multiple_of(to * BLK, BLK), BLK), :]
        dst = dq_out.at[:, pl.ds(pl.multiple_of((col * 2 + h) * HD, HD), HD)]

        @pl.when(to != col)
        def _():
            remote(src, dst, dq_send.at[h, to], dq_recv.at[h, col], (depth, to * 2 + z_lo)).start()

        @pl.when(to == col)
        def _():
            pltpu.make_async_copy(src, dst, dq_own.at[h]).start()

    def steps(n):
        def step(k):
            return pl.when(n == k)

        @step(1)
        def _():
            ring_step(3)

        @step(2)
        def _():
            ring_step(4)
            side_wait(4)

        @step(7)
        def _():
            side_wait(1)
            side_wait(3)
            for c in cross(1):
                c.wait_recv()

        @step(8)
        def _():
            for away in (4, 2, 6, 0):
                swap(away)

        @step(10)
        def _():
            swap_wait(4)
            sum_round(0, 1, 4)
            sum_round(1, -1, 4)

        @step(12 + z_lo)
        def _():
            swap(3)

        @step(13 + z_lo)
        def _():
            swap_wait(3)
            sum_round(1, 1, 3)
            sum_round(0, 1, 3)

        @step(14 + z_lo)
        def _():
            swap(5)

        @step(15 + z_lo)
        def _():
            down_three()

    def down_three():
        swap_wait(5)
        sum_round(0, -1, 3)
        sum_round(1, -1, 3)

    def join(part, value, halves, op):
        if halves == "ab":
            return op(part, value)
        if halves == "a":
            return jnp.concatenate([op(part[:, :BLK], value), part[:, BLK:]], axis=1)
        return jnp.concatenate([part[:, :BLK], op(part[:, BLK:], value)], axis=1)

    def place_of(n):
        order, h, u = tile_of(n)
        base = pl.multiple_of((4 * u + z_lo) * BLK, BLK)
        rows_q = pl.multiple_of(u * 2 * BLK, 2 * BLK)
        return order, h, base, rows_q

    def score_block(n, s_scr, block, top):
        k0, rows, halves, bound = block
        c0, cn = COLS[halves]
        order, h, base, rows_q = place_of(n)
        q = qg[order, 0, pl.ds(rows_q, 2 * BLK), :]
        s = dot_t(kv[0, h, pl.ds(pl.multiple_of(base + k0, 16), rows), :], q[c0 : c0 + cn])
        if bound is not None:
            key = lax.broadcasted_iota(jnp.int32, (rows, cn), 0)
            if bound == "low":
                low = jnp.maximum(last - span, WIN - 1 - base)
                keep = key > low[:, c0 : c0 + cn] - k0
            else:
                high = jnp.minimum(last, TOTAL + WIN - 1 - base)
                keep = key <= high[:, c0 : c0 + cn] - k0
            s = jnp.where(keep, s, NEG)
        s_scr[pl.ds(k0, rows), pl.ds(c0, cn)] = s
        return join(top, jnp.max(s, axis=0, keepdims=True), halves, jnp.maximum)

    lowest = jnp.full((1, 2 * BLK), NEG, F32)

    def tile(n, s_scr, top, after, s_after):
        order, h, base, rows_q = place_of(n)
        q = qg[order, 0, pl.ds(rows_q, 2 * BLK), :]
        g = qg[order, 1, pl.ds(rows_q, 2 * BLK), :]
        top = top * SCALE2
        sum_e = jnp.zeros((1, 2 * BLK), F32)
        sum_d = jnp.zeros((1, 2 * BLK), F32)
        for k0, rows, halves, bound in BLOCKS:
            c0, cn = COLS[halves]
            at = pl.multiple_of(base + k0, 16)
            dp = dot_t(kv[1, h, pl.ds(at, rows), :], g[c0 : c0 + cn])
            e = jnp.exp2(s_scr[pl.ds(k0, rows), pl.ds(c0, cn)] * SCALE2 - top[:, c0 : c0 + cn])
            sum_e = join(sum_e, jnp.sum(e, axis=0, keepdims=True), halves, jnp.add)
            sum_d = join(sum_d, jnp.sum(e * dp, axis=0, keepdims=True), halves, jnp.add)
            s_scr[pl.ds(k0, rows), pl.ds(c0, cn)] = e
            dp_scr[pl.ds(k0, rows), pl.ds(c0, cn)] = dp
        inv = 1.0 / sum_e
        rowdot = sum_d * inv
        new_top = lowest
        for block in BLOCKS:
            k0, rows, halves, bound = block
            c0, cn = COLS[halves]
            at = pl.multiple_of(base + k0, 16)
            p = s_scr[pl.ds(k0, rows), pl.ds(c0, cn)] * inv[:, c0 : c0 + cn]
            ds = p * (dp_scr[pl.ds(k0, rows), pl.ds(c0, cn)] - rowdot[:, c0 : c0 + cn])
            ds = ds.astype(BF16)
            ds_scr[pl.ds(k0, rows), pl.ds(c0, cn)] = ds
            new_top = score_block(after, s_after, block, new_top)
            acc[1, h, pl.ds(at, rows), :] += dot(p.astype(BF16), g[c0 : c0 + cn])
            acc[0, h, pl.ds(at, rows), :] += dot(ds, q[c0 : c0 + cn])
        dqt = dot(kt[h, :, pl.ds(base, TAIL)], ds_scr[...])
        dqs[h, pl.ds(rows_q, 2 * BLK), :] = (dqt.T * SCALE).astype(BF16)
        return new_top

    def before(n):
        steps(n)

        @pl.when(n >= 1)
        def _():
            for b in range(2):
                send_dq(n - 1, b)

    def pair(i, top):
        n = 2 * i
        before(n)
        top = tile(n, s_scr, top, n + 1, s_scr2)
        before(n + 1)
        return tile(n + 1, s_scr2, top, jnp.minimum(n + 2, 15), s_scr)

    first = lowest
    for block in BLOCKS:
        first = score_block(0, s_scr, block, first)
    lax.fori_loop(0, 8, pair, first)

    swap(1)
    swap(7)

    @pl.when(z_lo == 1)
    def _():
        down_three()

    swap_wait(2)
    swap_wait(6)
    sum_round(1, 1, 2)
    sum_round(0, 1, 2)
    for k in range(2):
        send_dq(15, k)
    sum_round(0, -1, 2)
    sum_round(1, -1, 2)
    swap_wait(1)
    sum_round(1, 1, 1)
    sum_round(0, 1, 1)
    swap_wait(7)
    sum_round(0, -1, 1)
    sum_round(1, -1, 1)
    swap_copy(z).wait_recv()
    for t, dst in enumerate((dk_out, dv_out)):
        value = chip_sum(t, z)
        for way in (-1, 1):
            sum_copy(t, way, 1).wait_recv()
            value += ring_in[2 * t + (1 if way > 0 else 0), 0].astype(F32)
        dst[...] = value.astype(BF16)

    for h in range(2):
        dst = dq_out.at[:, pl.ds(pl.multiple_of((col * 2 + h) * HD, HD), HD)]
        pltpu.make_async_copy(dqs.at[h, pl.ds(mine, BLK), :], dst, dq_own.at[h]).wait()
        for dx, dy in MOVES:
            to = ((x + dx) % SIDE) * SIDE + (y + dy) % SIDE
            src = dqs.at[h, pl.ds(pl.multiple_of(to * BLK, BLK), BLK), :]
            into = dq_out.at[:, pl.ds(pl.multiple_of((to * 2 + h) * HD, HD), HD)]
            remote(src, into, dq_send.at[h, to], dq_recv.at[h, to], at_xy(dx, dy)).wait()
    for f, (t, way, hops) in enumerate(FLOWS):
        for hop in range(hops):
            here = slot(t, z, core)
            ring_copy(f, hop, here, here).wait_send()
            side_copy(f, hop, here, here).wait_send()
    for t in range(2):
        here = slot(t, z, core)
        side_copy(4, t, here, here).wait_send()
    for order in range(2):
        for c in cross(order):
            c.wait_send()
    for target in range(RING):
        swap_copy(target).wait_send()
    for t, way, hops in FLOWS:
        for left in range(1, hops + 1):
            sum_copy(t, way, left).wait_send()


def on_device(queries, grad_out, key_states, value_states, offsets, windows):
    rows, width = queries.shape[1:]
    anywhere = pl.BlockSpec(memory_space=pl.ANY)
    vmem = pl.BlockSpec(memory_space=pltpu.VMEM)
    smem = pl.BlockSpec(memory_space=pltpu.SMEM)
    dma = pltpu.SemaphoreType.DMA
    dq, dk, dv = pl.pallas_call(
        fused_kernel,
        out_shape=(
            jax.ShapeDtypeStruct((rows, width), BF16),
            jax.ShapeDtypeStruct(key_states.shape, BF16),
            jax.ShapeDtypeStruct(key_states.shape, BF16),
        ),
        in_specs=[smem, smem] + [anywhere] * 4,
        out_specs=(anywhere, vmem, vmem),
        scratch_shapes=[
            pltpu.VMEM((2, 2, PEERS * BLK, HD), BF16),
            pltpu.VMEM((2, 2, PAD, HD), BF16),
            pltpu.VMEM((2, HD, PAD), BF16),
            pltpu.VMEM((2, 2, PAD, HD), F32),
            pltpu.VMEM((SPAN, 2 * BLK), F32),
            pltpu.VMEM((SPAN, 2 * BLK), F32),
            pltpu.VMEM((SPAN, 2 * BLK), F32),
            pltpu.VMEM((TAIL, 2 * BLK), BF16),
            pltpu.VMEM((2, PEERS * BLK, HD), BF16),
            pltpu.VMEM((RING, 2, SHARD, HD), BF16),
            pltpu.VMEM((RING, 2, SHARD, HD), BF16),
            pltpu.VMEM((4, 4, SHARD, HD), BF16),
            pltpu.VMEM((4, 4, SHARD, HD), BF16),
            dma((2, 2, 15)), dma((2, 2, 15)), dma((3, 2)),
            dma((4, 4)), dma((4, 4)), dma((5, 4)), dma((5, 4)),
            dma((2, 16)), dma((2, 16)), dma((2,)),
            dma((8,)), dma((8,)), dma((4, 4)), dma((4, 4)),
        ],
        compiler_params=pltpu.CompilerParams(
            collective_id=0, has_side_effects=True, vmem_limit_bytes=56 << 20
        ),
    )(
        offsets, windows, queries.reshape(rows, width), grad_out.reshape(rows, width),
        key_states, value_states,
    )
    return dq.reshape(1, rows, width), dk, dv


def solution(mesh):
    in_specs = (
        P("depth", "seq", None),
        P("depth", "seq", None),
        P("depth", "seq"),
        P("depth", "seq"),
        P(),
        P(),
    )
    out_specs = (P("depth", "seq", None), P("depth", "seq"), P("depth", "seq"))
    return jax.shard_map(
        on_device, mesh=mesh, in_specs=in_specs, out_specs=out_specs, check_vma=False
    )
```

```python
import functools
import math

import jax
import jax.numpy as jnp
from jax import lax
from jax.experimental import pallas as pl
from jax.experimental.pallas import tpu as pltpu
from jax.sharding import PartitionSpec as P

HD = 128
WIN = 1024
BLK = 128
SIDE = 4
PEERS = SIDE * SIDE
RING = 8
SHARD = 512
TOTAL = 4096
PAD = TOTAL + WIN + BLK
SPAN = WIN + 3 * BLK + 16
TAIL = 1536
NEG = -1e30
SCALE = 1.0 / math.sqrt(HD)
SCALE2 = SCALE * math.log2(math.e)
F32 = jnp.float32
BF16 = jnp.bfloat16
MESH = pl.DeviceIdType.MESH

BLOCKS = (
    (0, 256, "a", "low"),
    (256, 384, "ab", "low"),
    (640, 384, "ab", "low"),
    (1024, 144, "ab", "high"),
    (1168, 112, "b", None),
    (1280, 144, "b", "high"),
)
COLS = {"a": (0, BLK), "b": (BLK, BLK), "ab": (0, 2 * BLK)}
MOVES = (
    (0, 1), (1, 0), (0, 3), (3, 0), (1, 1), (3, 3), (1, 3), (3, 1),
    (0, 2), (2, 0), (2, 1), (1, 2), (2, 3), (3, 2), (2, 2),
)
FLOWS = ((0, 1, 4), (1, -1, 4), (0, -1, 3), (1, 1, 3))
HOPS = {(t, way): hops for t, way, hops in FLOWS}


def dot_t(a, b):
    return lax.dot_general(a, b, (((1,), (1,)), ((), ())), preferred_element_type=F32)


def dot(a, b):
    return jnp.dot(a, b, preferred_element_type=F32)


def fused_kernel(
    off_ref, win_ref, q_in, g_in, k_in, v_in,
    dq_out, dk_out, dv_out,
    qg, kv, kt, acc, s_scr, s_scr2, dp_scr, ds_scr, dqs, sib_out, sib_in, ring_out, ring_in,
    x_send, x_recv, own_sem, ag_send, ag_recv, sb_send, sb_recv, dq_send, dq_recv, dq_own,
    ss_send, ss_recv, rs_send, rs_recv,
):
    depth = lax.axis_index("depth")
    seq = lax.axis_index("seq")
    core = depth % 2
    z_lo = seq % 2
    col = seq // 2
    x = col // SIDE
    y = col % SIDE
    z = (depth // 2) * 2 + z_lo

    def at_xy(dx, dy):
        return (depth, (((x + dx) % SIDE) * SIDE + (y + dy) % SIDE) * 2 + z_lo)

    def at_z(to):
        return ((to // 2) * 2 + core, col * 2 + to % 2)

    up = at_z((z + 1) % RING)
    down = at_z((z + RING - 1) % RING)
    sibling = (depth + 1 - 2 * core, seq)

    barrier = pltpu.get_barrier_semaphore()
    partners = [at_xy(*m) for m in MOVES] + [up, down, sibling]
    for dev in partners:
        pl.semaphore_signal(barrier, inc=1, device_id=dev, device_id_type=MESH)
    pl.semaphore_wait(barrier, len(partners))

    def remote(src, dst, send, recv, dev):
        return pltpu.make_async_remote_copy(
            src_ref=src, dst_ref=dst, send_sem=send, recv_sem=recv, device_id=dev, device_id_type=MESH
        )

    def slot(t, origin, side):
        row = pl.multiple_of(WIN + ((origin // 2) * 2 + side) * SHARD, SHARD)
        return kv.at[t, origin % 2, pl.ds(row, SHARD), :]

    own_kv = (k_in, v_in)

    def along(way):
        return up if way > 0 else down

    def ring_copy(f, hop, src, dst):
        return remote(src, dst, ag_send.at[f, hop], ag_recv.at[f, hop], along(FLOWS[f][1]))

    def side_copy(f, hop, src, dst):
        return remote(src, dst, sb_send.at[f, hop], sb_recv.at[f, hop], sibling)

    def send_own():
        for f, (t, way, hops) in enumerate(FLOWS):
            ring_copy(f, 0, own_kv[t], slot(t, z, core)).start()
        for t in range(2):
            side_copy(4, t, own_kv[t], slot(t, z, core)).start()

    def turn(origin, side):
        row = pl.multiple_of(WIN + ((origin // 2) * 2 + side) * SHARD, SHARD)
        kt[origin % 2, :, pl.ds(row, SHARD)] = kv[0, origin % 2, pl.ds(row, SHARD), :].T

    def origin_of(way, away):
        return (z + RING - way * away) % RING

    def ring_step(away):
        flows = [(f, t, way, hops) for f, (t, way, hops) in enumerate(FLOWS) if away <= hops]
        for f, t, way, hops in flows:
            here = slot(t, origin_of(way, away), core)
            ring_copy(f, away - 1, here, here).wait_recv()
            if away < hops:
                ring_copy(f, away, here, here).start()
            side_copy(f, away - 1, here, here).start()
        for f, t, way, hops in flows:
            if t == 0:
                turn(origin_of(way, away), core)

    def side_wait(away):
        if away == 0:
            for t in range(2):
                there = slot(t, z, 1 - core)
                side_copy(4, t, there, there).wait_recv()
            turn(z, 1 - core)
            return
        for f, (t, way, hops) in enumerate(FLOWS):
            if away <= hops:
                there = slot(t, origin_of(way, away), 1 - core)
                side_copy(f, away - 1, there, there).wait_recv()
                if t == 0:
                    turn(origin_of(way, away), 1 - core)

    heads = (z_lo, 1 - z_lo)

    mine = pl.multiple_of(col * BLK, BLK)

    def cross(order):
        h = heads[order]
        for i, (dx, dy) in enumerate(MOVES):
            for t, src in enumerate((q_in, g_in)):
                to = ((x + dx) % SIDE) * SIDE + (y + dy) % SIDE
                yield remote(
                    src.at[:, pl.ds(pl.multiple_of((to * 2 + h) * HD, HD), HD)],
                    qg.at[order, t, pl.ds(mine, BLK), :],
                    x_send.at[order, t, i],
                    x_recv.at[order, t, i],
                    at_xy(dx, dy),
                )

    local = []
    for t in range(2):
        local.append(pltpu.make_async_copy(own_kv[t], slot(t, z, core), own_sem.at[0, t]))
    for order in range(2):
        for t, src in enumerate((q_in, g_in)):
            local.append(
                pltpu.make_async_copy(
                    src.at[:, pl.ds(pl.multiple_of((col * 2 + heads[order]) * HD, HD), HD)],
                    qg.at[order, t, pl.ds(mine, BLK), :],
                    own_sem.at[1 + order, t],
                )
            )

    send_own()
    for c in local:
        c.start()
    for order in range(2):
        for c in cross(order):
            c.start()
    for h in range(2):
        for t in range(2):
            kv[t, h, pl.ds(0, WIN), :] = jnp.zeros((WIN, HD), BF16)
            kv[t, h, pl.ds(WIN + TOTAL, BLK), :] = jnp.zeros((BLK, HD), BF16)
        kt[h, :, pl.ds(0, WIN)] = jnp.zeros((HD, WIN), BF16)
        kt[h, :, pl.ds(WIN + TOTAL, BLK)] = jnp.zeros((HD, BLK), BF16)
    acc[...] = jnp.zeros_like(acc)
    ds_scr[...] = jnp.zeros_like(ds_scr)
    local[0].wait()
    turn(z, core)
    ring_step(1)
    ring_step(2)
    side_wait(0)
    side_wait(2)
    for c in local[1:]:
        c.wait()
    for c in cross(0):
        c.wait_recv()

    quarter = depth // 2

    def partial(t, target, side):
        row = pl.multiple_of(WIN + ((target // 2) * 2 + side) * SHARD, SHARD)
        value = acc[t, target % 2, pl.ds(row, SHARD), :]
        return value * SCALE if t == 0 else value

    def swap_copy(target):
        return remote(
            sib_out.at[target], sib_in.at[target], ss_send.at[target], ss_recv.at[target], sibling
        )

    def swap(away):
        target = (z + away) % RING
        for t in range(2):
            sib_out[target, t] = partial(t, target, 1 - core).astype(BF16)
        swap_copy(target).start()

    def chip_sum(t, target):
        return partial(t, target, core) + sib_in[target, t].astype(F32)

    def sum_copy(t, way, left):
        f = 2 * t + (1 if way > 0 else 0)
        return remote(
            ring_out.at[f, left - 1], ring_in.at[f, left - 1],
            rs_send.at[f, left - 1], rs_recv.at[f, left - 1], along(way),
        )

    def sum_round(t, way, left):
        value = chip_sum(t, (z + RING + way * left) % RING)
        if left < HOPS[t, way]:
            sum_copy(t, way, left + 1).wait_recv()
            value += ring_in[2 * t + (1 if way > 0 else 0), left].astype(F32)
        ring_out[2 * t + (1 if way > 0 else 0), left - 1] = value.astype(BF16)
        sum_copy(t, way, left).start()

    def swap_wait(away):
        swap_copy((z + away) % RING).wait_recv()

    shift = off_ref[depth]
    span = win_ref[depth]
    lane = lax.broadcasted_iota(jnp.int32, (1, 2 * BLK), 1)
    place = lane + jnp.where(lane >= BLK, BLK, 0)
    last = place + WIN + shift

    def tile_of(n):
        order = n // 8
        h = jnp.where(order == 0, heads[0], heads[1])
        return order, h, (2 * quarter + n + order * (2 + z_lo)) % 8

    def send_dq(group, k):
        m = (k + col) % 2
        order, h, u = tile_of(group)
        to = 2 * u + m
        src = dqs.at[h, pl.ds(pl.multiple_of(to * BLK, BLK), BLK), :]
        dst = dq_out.at[:, pl.ds(pl.multiple_of((col * 2 + h) * HD, HD), HD)]

        @pl.when(to != col)
        def _():
            remote(src, dst, dq_send.at[h, to], dq_recv.at[h, col], (depth, to * 2 + z_lo)).start()

        @pl.when(to == col)
        def _():
            pltpu.make_async_copy(src, dst, dq_own.at[h]).start()

    def steps(n):
        def step(k):
            return pl.when(n == k)

        @step(1)
        def _():
            ring_step(3)

        @step(2)
        def _():
            side_wait(1)
            side_wait(3)
            ring_step(4)
            side_wait(4)

        @step(7)
        def _():
            for c in cross(1):
                c.wait_recv()

        @step(8)
        def _():
            for away in (4, 2, 6, 0):
                swap(away)

        @step(9)
        def _():
            swap_wait(4)
            sum_round(0, 1, 4)
            sum_round(1, -1, 4)

        @step(12 + z_lo)
        def _():
            swap(3)

        @step(13 + z_lo)
        def _():
            swap_wait(3)
            sum_round(1, 1, 3)
            sum_round(0, 1, 3)

        @step(14 + z_lo)
        def _():
            swap(5)

        @step(15)
        def _():
            down_three()

    def down_three():
        swap_wait(5)
        sum_round(0, -1, 3)
        sum_round(1, -1, 3)

    def join(part, value, halves, op):
        if halves == "ab":
            return op(part, value)
        if halves == "a":
            return jnp.concatenate([op(part[:, :BLK], value), part[:, BLK:]], axis=1)
        return jnp.concatenate([part[:, :BLK], op(part[:, BLK:], value)], axis=1)

    def place_of(n):
        order, h, u = tile_of(n)
        base = pl.multiple_of((4 * u + z_lo) * BLK, BLK)
        rows_q = pl.multiple_of(u * 2 * BLK, 2 * BLK)
        return order, h, base, rows_q

    def score_block(n, s_scr, block, top):
        k0, rows, halves, bound = block
        c0, cn = COLS[halves]
        order, h, base, rows_q = place_of(n)
        q = qg[order, 0, pl.ds(rows_q, 2 * BLK), :]
        s = dot_t(kv[0, h, pl.ds(pl.multiple_of(base + k0, 16), rows), :], q[c0 : c0 + cn])
        if bound is not None:
            key = lax.broadcasted_iota(jnp.int32, (rows, cn), 0)
            if bound == "low":
                low = jnp.maximum(last - span, WIN - 1 - base)
                keep = key > low[:, c0 : c0 + cn] - k0
            else:
                high = jnp.minimum(last, TOTAL + WIN - 1 - base)
                keep = key <= high[:, c0 : c0 + cn] - k0
            s = jnp.where(keep, s, NEG)
        s_scr[pl.ds(k0, rows), pl.ds(c0, cn)] = s
        return join(top, jnp.max(s, axis=0, keepdims=True), halves, jnp.maximum)

    lowest = jnp.full((1, 2 * BLK), NEG, F32)

    def tile(n, s_scr, top, after, s_after):
        order, h, base, rows_q = place_of(n)
        q = qg[order, 0, pl.ds(rows_q, 2 * BLK), :]
        g = qg[order, 1, pl.ds(rows_q, 2 * BLK), :]
        top = top * SCALE2
        sum_e = jnp.zeros((1, 2 * BLK), F32)
        sum_d = jnp.zeros((1, 2 * BLK), F32)
        for k0, rows, halves, bound in BLOCKS:
            c0, cn = COLS[halves]
            at = pl.multiple_of(base + k0, 16)
            dp = dot_t(kv[1, h, pl.ds(at, rows), :], g[c0 : c0 + cn])
            e = jnp.exp2(s_scr[pl.ds(k0, rows), pl.ds(c0, cn)] * SCALE2 - top[:, c0 : c0 + cn])
            sum_e = join(sum_e, jnp.sum(e, axis=0, keepdims=True), halves, jnp.add)
            sum_d = join(sum_d, jnp.sum(e * dp, axis=0, keepdims=True), halves, jnp.add)
            s_scr[pl.ds(k0, rows), pl.ds(c0, cn)] = e
            dp_scr[pl.ds(k0, rows), pl.ds(c0, cn)] = dp
        inv = 1.0 / sum_e
        rowdot = sum_d * inv
        new_top = lowest
        for block in BLOCKS:
            k0, rows, halves, bound = block
            c0, cn = COLS[halves]
            at = pl.multiple_of(base + k0, 16)
            p = s_scr[pl.ds(k0, rows), pl.ds(c0, cn)] * inv[:, c0 : c0 + cn]
            ds = p * (dp_scr[pl.ds(k0, rows), pl.ds(c0, cn)] - rowdot[:, c0 : c0 + cn])
            ds = ds.astype(BF16)
            ds_scr[pl.ds(k0, rows), pl.ds(c0, cn)] = ds
            if s_after is not None:
                new_top = score_block(after, s_after, block, new_top)
            acc[1, h, pl.ds(at, rows), :] += dot(p.astype(BF16), g[c0 : c0 + cn])
            acc[0, h, pl.ds(at, rows), :] += dot(ds, q[c0 : c0 + cn])
        dqt = dot(kt[h, :, pl.ds(base, TAIL)], ds_scr[...])
        dqs[h, pl.ds(rows_q, 2 * BLK), :] = (dqt.T * (2 * SCALE)).astype(BF16)
        return new_top

    def before(n):
        steps(n)

        @pl.when(n >= 1)
        def _():
            for b in range(2):
                send_dq(n - 1, b)

    def pair(i, top):
        n = 2 * i
        before(n)
        top = tile(n, s_scr, top, n + 1, s_scr2)
        before(n + 1)
        return tile(n + 1, s_scr2, top, n + 2, s_scr)

    first = lowest
    for block in BLOCKS:
        first = score_block(0, s_scr, block, first)
    top = lax.fori_loop(0, 7, pair, first)
    before(jnp.int32(14))
    top = tile(jnp.int32(14), s_scr, top, jnp.int32(15), s_scr2)
    before(jnp.int32(15))
    tile(jnp.int32(15), s_scr2, top, None, None)

    swap(1)
    swap(7)

    swap_wait(2)
    swap_wait(6)
    sum_round(1, 1, 2)
    sum_round(0, 1, 2)
    for k in range(2):
        send_dq(15, k)
    sum_round(0, -1, 2)
    sum_round(1, -1, 2)
    swap_wait(1)
    sum_round(1, 1, 1)
    sum_round(0, 1, 1)
    swap_wait(7)
    sum_round(0, -1, 1)
    sum_round(1, -1, 1)
    swap_copy(z).wait_recv()
    for t, dst in enumerate((dk_out, dv_out)):
        value = chip_sum(t, z)
        for way in (-1, 1):
            sum_copy(t, way, 1).wait_recv()
            value += ring_in[2 * t + (1 if way > 0 else 0), 0].astype(F32)
        dst[...] = (value * 2).astype(BF16)

    for h in range(2):
        dst = dq_out.at[:, pl.ds(pl.multiple_of((col * 2 + h) * HD, HD), HD)]
        pltpu.make_async_copy(dqs.at[h, pl.ds(mine, BLK), :], dst, dq_own.at[h]).wait()
        for dx, dy in MOVES:
            to = ((x + dx) % SIDE) * SIDE + (y + dy) % SIDE
            src = dqs.at[h, pl.ds(pl.multiple_of(to * BLK, BLK), BLK), :]
            into = dq_out.at[:, pl.ds(pl.multiple_of((to * 2 + h) * HD, HD), HD)]
            remote(src, into, dq_send.at[h, to], dq_recv.at[h, to], at_xy(dx, dy)).wait()
    for f, (t, way, hops) in enumerate(FLOWS):
        for hop in range(hops):
            here = slot(t, z, core)
            ring_copy(f, hop, here, here).wait_send()
            side_copy(f, hop, here, here).wait_send()
    for t in range(2):
        here = slot(t, z, core)
        side_copy(4, t, here, here).wait_send()
    for order in range(2):
        for c in cross(order):
            c.wait_send()
    for target in range(RING):
        swap_copy(target).wait_send()
    for t, way, hops in FLOWS:
        for left in range(1, hops + 1):
            sum_copy(t, way, left).wait_send()


def on_device(queries, grad_out, key_states, value_states, offsets, windows):
    rows, width = queries.shape[1:]
    anywhere = pl.BlockSpec(memory_space=pl.ANY)
    vmem = pl.BlockSpec(memory_space=pltpu.VMEM)
    smem = pl.BlockSpec(memory_space=pltpu.SMEM)
    dma = pltpu.SemaphoreType.DMA
    dq, dk, dv = pl.pallas_call(
        fused_kernel,
        out_shape=(
            jax.ShapeDtypeStruct((rows, width), BF16),
            jax.ShapeDtypeStruct(key_states.shape, BF16),
            jax.ShapeDtypeStruct(key_states.shape, BF16),
        ),
        in_specs=[smem, smem] + [anywhere] * 4,
        out_specs=(anywhere, vmem, vmem),
        scratch_shapes=[
            pltpu.VMEM((2, 2, PEERS * BLK, HD), BF16),
            pltpu.VMEM((2, 2, PAD, HD), BF16),
            pltpu.VMEM((2, HD, PAD), BF16),
            pltpu.VMEM((2, 2, PAD, HD), F32),
            pltpu.VMEM((SPAN, 2 * BLK), F32),
            pltpu.VMEM((SPAN, 2 * BLK), F32),
            pltpu.VMEM((SPAN, 2 * BLK), F32),
            pltpu.VMEM((TAIL, 2 * BLK), BF16),
            pltpu.VMEM((2, PEERS * BLK, HD), BF16),
            pltpu.VMEM((RING, 2, SHARD, HD), BF16),
            pltpu.VMEM((RING, 2, SHARD, HD), BF16),
            pltpu.VMEM((4, 4, SHARD, HD), BF16),
            pltpu.VMEM((4, 4, SHARD, HD), BF16),
            dma((2, 2, 15)), dma((2, 2, 15)), dma((3, 2)),
            dma((4, 4)), dma((4, 4)), dma((5, 4)), dma((5, 4)),
            dma((2, 16)), dma((2, 16)), dma((2,)),
            dma((8,)), dma((8,)), dma((4, 4)), dma((4, 4)),
        ],
        compiler_params=pltpu.CompilerParams(
            collective_id=0, has_side_effects=True, vmem_limit_bytes=56 << 20
        ),
    )(
        offsets, windows, queries.reshape(rows, width), grad_out.reshape(rows, width),
        key_states, value_states,
    )
    half = jnp.asarray(0.5, BF16)
    return (dq * half).reshape(1, rows, width), dk * half, dv * half


def solution(mesh):
    in_specs = (
        P("depth", "seq", None),
        P("depth", "seq", None),
        P("depth", "seq"),
        P("depth", "seq"),
        P(),
        P(),
    )
    out_specs = (P("depth", "seq", None), P("depth", "seq"), P("depth", "seq"))
    return jax.shard_map(
        on_device, mesh=mesh, in_specs=in_specs, out_specs=out_specs, check_vma=False
    )
```
